32 devices in a mesh: facet: 4 (over z), col: 8 (over y, x, core).
Axes of the slice: x: 2, y: 2, z: 4, core: 2. Of those that a mesh axis runs over, the one named last changes fastest.
Arguments:
- sky_re: bfloat16 [4, 4096, 4096], P('facet', None, 'col'), may hold values from -6 to 6
- sky_im: bfloat16 [4, 4096, 4096], P('facet', None, 'col'), may hold values from -6 to 6
- col_offsets: int32 [2], replicated, may hold values from 0 to 65280
- sub_offsets: int32 [4], replicated, may hold values from 0 to 65280
- kernel: float32 [16, 8], replicated, may hold values from 0.05 to 1
- vis_count: int32 [4, 32], P('facet', 'col'), may hold values from 0 to 128, as said below
- cell_index: int32 [2, 4, 32, 128], P(None, 'facet', 'col'), may hold values from 0 to 248
- frac_index: int32 [2, 4, 32, 128], P(None, 'facet', 'col'), may hold values from 0 to 15
Outputs:
- vis_re: float32 [4, 32, 128], P('facet', 'col')
- vis_im: float32 [4, 32, 128], P('facet', 'col')
The draws below stay inside these ranges and needn't reach their ends.
Inputs may be any that keep to these rules, and one draw needn't show every extreme that they name: Within each subgrid the blocks with visibilities come first and block 0 holds 128; in some subgrid all 32 blocks hold visibilities; a block's visibilities fill its first vis_count slots.
All inputs are finite; a program needn't handle non-finite values.
Results may differ from the reference program's by a relative error of at most 0.0037.
Values may be sent and summed in bfloat16 or wider, within the bound.
A program may use at most 64 MiB of HBM per device.

```python
import math
import jax
import jax.numpy as jnp
from jax import lax

N_IMG = 65536
M = 4096
S = 256
KS = 8
OS = 16
SCOL = 2
VB = 128
NSUB = 4
BLK_SUB = 32
N_FACET = 4


def draw_vis_count(key, part):
    key_full, key_live, key_counts = jax.random.split(jax.random.fold_in(key, 11), 3)
    full_index = jax.random.randint(key_full, (), 0, NSUB)
    raw_draws = jax.random.randint(key_live, (NSUB,), 1, BLK_SUB + 1)
    live_blocks = jnp.maximum(1, raw_draws * raw_draws // BLK_SUB)
    live_blocks = jnp.where(jnp.arange(NSUB) == full_index, BLK_SUB, live_blocks)
    counts = jax.random.randint(key_counts, (NSUB, BLK_SUB), 1, VB + 1)
    block_ids = jnp.arange(BLK_SUB)[None, :]
    counts = jnp.where(block_ids == 0, VB, counts)
    return jnp.where(block_ids < live_blocks[:, None], counts, 0).astype(jnp.int32)


def place_ends(drawn, own_key, smallest, top_value):
    shape = drawn.shape
    index_at = [jax.random.randint(jax.random.fold_in(own_key, axis), (), 0, shape[axis]) for axis in range(len(shape))]
    drawn = drawn.at[tuple(index_at)].set(smallest)
    longest = shape.index(max(shape))
    index_at[longest] = (index_at[longest] + 1) % shape[longest]
    return drawn.at[tuple(index_at)].set(top_value)


def level_of(rng, extent, shards, smallest, high):
    def one(axis_at, shards_of):
        draws = jax.random.uniform(jax.random.fold_in(jax.random.fold_in(rng, 6), axis_at), (shards_of,), jnp.float32, smallest / len(shards), high / len(shards))
        return jnp.repeat(jnp.exp(draws), extent[axis_at] // shards_of).reshape((-1,) + (1,) * (len(extent) - axis_at - 1))

    level = one(*shards[0])
    for cut in shards[1:]:
        level = level * one(*cut)
    return level


def centred(stream_key, shape, scale, bound, cuts=(), kind=jnp.bfloat16):
    array = jax.random.normal(stream_key, shape, jnp.float32) * scale
    if len(cuts) > 0:
        array = level_of(stream_key, shape, cuts, -0.22, 0.18) * array
    return jnp.clip(array, min=-bound, max=bound).astype(kind)


def setup_inputs(seed: int = 0) -> dict:
    arg_keys = jax.random.split(jax.random.key(seed), 9)
    sky_re = centred(arg_keys[0], (N_FACET, M, M), 1.0, 6.0, ((0, 4), (2, 8)))
    sky_im = centred(arg_keys[1], (N_FACET, M, M), 1.0, 6.0, ((0, 4), (2, 8)))
    col_offsets = jax.random.randint(arg_keys[2], (SCOL,), 0, N_IMG - S + 1).astype(jnp.int32)
    sub_offsets = place_ends(jax.random.randint(arg_keys[3], (NSUB,), 0, N_IMG - S + 1), jax.random.fold_in(arg_keys[3], 1), 0, N_IMG - S).astype(jnp.int32)
    kernel = jnp.clip(jnp.exp(jax.random.uniform(arg_keys[4], (OS, KS), jnp.float32, math.log(0.05), math.log(1.0))), 0.05, 1.0)
    vis_count = draw_vis_count(jax.random.fold_in(arg_keys[8], 71), 0)
    cell_index = place_ends(jax.random.randint(arg_keys[6], (2, NSUB, BLK_SUB, VB), 0, S - KS + 1), jax.random.fold_in(arg_keys[6], 1), 0, S - KS).astype(jnp.int32)
    frac_index = place_ends(jax.random.randint(arg_keys[7], (2, NSUB, BLK_SUB, VB), 0, OS), jax.random.fold_in(arg_keys[7], 1), 0, OS - 1).astype(jnp.int32)
    return {"sky_re": sky_re, "sky_im": sky_im, "col_offsets": col_offsets, "sub_offsets": sub_offsets, "kernel": kernel, "vis_count": vis_count, "cell_index": cell_index, "frac_index": frac_index}


def modular_product(left_ints, right_ints):
    upper_part = right_ints // 256
    lower_part = right_ints % 256
    product = left_ints[:, None] * upper_part[None, :] % N_IMG
    product = product * 256 % N_IMG
    return (product + left_ints[:, None] * lower_part[None, :]) % N_IMG

def cos_sin(left_ints, right_ints, factor):
    angles = modular_product(left_ints, right_ints).astype(jnp.float32) * (2.0 * math.pi / N_IMG)
    return (jnp.cos(angles) * factor, jnp.sin(angles) * factor)

def first_axis(facet_image, table, local_cols):
    product = jnp.dot(table, facet_image, preferred_element_type=jnp.float32)
    real_part = product[:S, :local_cols] + product[S:, local_cols:]
    imag_part = product[:S, local_cols:] - product[S:, :local_cols]
    return jnp.stack([real_part, imag_part]).astype(jnp.bfloat16)

def second_axis(band_rows, starts, anchor, second_table):
    mod_cos, mod_sin = cos_sin(starts, anchor, 1.0)
    shifted_re = band_rows[0][None] * mod_cos[:, None] + band_rows[1][None] * mod_sin[:, None]
    shifted_im = band_rows[1][None] * mod_cos[:, None] - band_rows[0][None] * mod_sin[:, None]
    stacked = jnp.concatenate([shifted_re, shifted_im], axis=0).astype(jnp.bfloat16)
    per_column = starts.shape[0]
    row_count = band_rows.shape[1]
    product = jnp.dot(stacked.reshape(2 * per_column * row_count, -1), second_table, preferred_element_type=jnp.float32)
    product = product.reshape(2, per_column, row_count, 2 * S)
    term_re = product[0, :, :, :S] + product[1, :, :, S:]
    term_im = product[1, :, :, :S] - product[0, :, :, S:]
    return jnp.concatenate([term_re, term_im], axis=2)

def lookup(frac_ints, kernel):
    table_rows = jnp.arange(kernel.shape[0], dtype=jnp.int32)
    matches = frac_ints[..., None] == table_rows
    return lax.optimization_barrier(jnp.sum(jnp.where(matches[..., None], kernel, 0.0), axis=-2))

def reference(sky_re, sky_im, col_offsets, sub_offsets, kernel, vis_count, cell_index, frac_index):
    spatial = jnp.arange(M, dtype=jnp.int32)
    spectral = jnp.arange(S, dtype=jnp.int32)
    per_column = NSUB // SCOL
    first_tables = []
    for column in range(SCOL):
        cos_part, sin_part = cos_sin(col_offsets[column] + spectral, spatial, 1.0 / math.sqrt(M))
        first_tables.append(jnp.concatenate([cos_part, sin_part], axis=0).astype(jnp.bfloat16))

    def facet_step(running, inputs):
        real_part, imag_part, facet_index = inputs
        facet_image = jnp.concatenate([real_part, imag_part], axis=1)
        anchor = facet_index * M + spatial
        cos_tab, sin_tab = cos_sin(anchor, spectral, 1.0 / math.sqrt(M * N_FACET))
        second_table = jnp.concatenate([cos_tab, sin_tab], axis=1).astype(jnp.bfloat16)
        column_terms = []
        for column in range(SCOL):
            band_rows = first_axis(facet_image, first_tables[column], M)
            starts = sub_offsets[column * per_column:(column + 1) * per_column]
            column_terms.append(second_axis(band_rows, starts, anchor, second_table))
        return (running + jnp.concatenate(column_terms, axis=0), None)
    initial = jnp.zeros((NSUB, S, 2 * S), jnp.float32)
    subgrids, _ = lax.scan(facet_step, initial, (sky_re, sky_im, jnp.arange(N_FACET, dtype=jnp.int32)))
    subgrids = subgrids.astype(jnp.bfloat16)
    offsets = jnp.arange(KS, dtype=jnp.int32)
    slot_ids = jnp.arange(VB, dtype=jnp.int32)

    def one_subgrid(inputs):
        subgrid, cell_rows, frac_rows, counts = inputs

        def one_block(block_inputs):
            cell_block, frac_block, slot_count = block_inputs
            row_taps = lookup(frac_block[0], kernel).astype(jnp.bfloat16)
            row_taps = lax.optimization_barrier(row_taps).astype(jnp.float32)
            col_taps = lookup(frac_block[1], kernel)
            gathered = jnp.take(subgrid, cell_block[0][:, None] + offsets, axis=0).astype(jnp.float32)
            row_sum = jnp.einsum('va,vac->vc', row_taps, gathered, precision=lax.Precision.HIGHEST)
            col_ids = cell_block[1][:, None] + offsets
            picked_re = jnp.take_along_axis(row_sum[:, :S], col_ids, axis=1)
            picked_im = jnp.take_along_axis(row_sum[:, S:], col_ids, axis=1)
            in_block = slot_ids < slot_count
            vis_real = jnp.where(in_block, lax.optimization_barrier(jnp.sum(picked_re * col_taps, axis=1)), 0.0)
            vis_imag = jnp.where(in_block, lax.optimization_barrier(jnp.sum(picked_im * col_taps, axis=1)), 0.0)
            return (vis_real, vis_imag)
        return lax.map(one_block, (jnp.moveaxis(cell_rows, 1, 0), jnp.moveaxis(frac_rows, 1, 0), counts))
    vis_real, vis_imag = lax.map(one_subgrid, (subgrids, jnp.moveaxis(cell_index, 1, 0), jnp.moveaxis(frac_index, 1, 0), vis_count))
    return (vis_real, vis_imag)
```

```python
import functools
import math

import jax
import jax.numpy as jnp
from jax import lax
from jax.experimental import pallas as pl
from jax.experimental.pallas import tpu as pltpu
from jax.sharding import PartitionSpec as P

N_IMG = 65536
S = 256
SCOL = 2
LANES = 128
F32 = jnp.float32
BF16 = jnp.bfloat16


def iota(shape, dim):
    return lax.broadcasted_iota(jnp.int32, shape, dim)


def unit(points, period):
    quarter = period // 4
    quad = (points + quarter // 2) >> (quarter.bit_length() - 1)
    x = (points - quad * quarter).astype(F32) * (2.0 * math.pi / period)
    x2 = x * x
    s = x2 * (1.0 / 362880) - 1.0 / 5040
    s = x2 * s + 1.0 / 120
    s = x2 * s - 1.0 / 6
    s = x * (x2 * s + 1.0)
    c = x2 * (1.0 / 40320) - 1.0 / 720
    c = x2 * c + 1.0 / 24
    c = x2 * c - 0.5
    c = x2 * c + 1.0
    odd = (quad & 1) != 0
    cos = jnp.where(odd, s, c)
    sin = jnp.where(odd, c, s)
    cos = jnp.where(((quad + 1) & 2) != 0, -cos, cos)
    sin = jnp.where((quad & 2) != 0, -sin, sin)
    return cos, sin


def product(left, right, period):
    upper = (left * (right >> 8)) & (period - 1)
    return (upper * 256 + left * (right & 255)) & (period - 1)


def times(left, right):
    return (
        left[0] * right[0] - left[1] * right[1],
        left[0] * right[1] + left[1] * right[0],
    )


def exclusive(left, right, count):
    total, bit = 0, 1
    while bit < count:
        total = total + ((left // bit) % 2 + (right // bit) % 2) % 2 * bit
        bit *= 2
    return total


def each(count, step):
    if count <= 16:
        for index in range(count):
            step(index)
    else:

        def once(index, carry):
            step(index)
            return carry

        lax.fori_loop(0, count, once, 0)


def body(
    dims,
    coff_ref,
    soff_ref,
    kern_ref,
    count_ref,
    cell_ref,
    frac_ref,
    re_hbm,
    im_hbm,
    vis_ref,
    sky,
    table_a,
    table_b,
    state,
    prod,
    base,
    shift_tab,
    table2,
    stacked,
    bands,
    bsend,
    cells,
    idx,
    idx_all,
    row_r,
    row_t,
    col_r,
    col_t,
    weights,
    vsend,
    vrecv,
    sky_sem,
    band_sem,
    isend_sem,
    irecv_sem,
    vsend_sem,
    vrecv_sem,
):
    n_f, n_c, pixels, cols, subs, blocks, slots, chunks, ksize, over = dims
    per = subs // SCOL
    n_p = n_c // SCOL
    half = S // 2
    rows = 64
    f = lax.axis_index("facet")
    c = lax.axis_index("col")
    core = lax.rem(c, SCOL)
    chip = c // SCOL
    side = f // per
    depth = pixels // chunks

    loads = []
    for t in range(chunks):
        for index, src in enumerate((re_hbm, im_hbm)):
            copy = pltpu.make_async_copy(
                src.at[0, pl.ds(t * depth, depth)],
                sky.at[index, pl.ds(t * depth, depth)],
                sky_sem.at[t, index],
            )
            copy.start()
            loads.append(copy)

    barrier = pltpu.get_barrier_semaphore()
    everyone = n_f * n_c

    def greet(step):
        other = lax.rem(f * n_c + c + 1 + step, everyone)
        pl.semaphore_signal(
            barrier, inc=1, device_id={"facet": other // n_c, "col": lax.rem(other, n_c)}
        )

    each(everyone - 1, greet)

    jrow = iota((rows, LANES), 0)
    lane = iota((rows, LANES), 1)
    base[0], base[1] = unit(jrow * lane, N_IMG)
    base[2], base[3] = unit(jrow * LANES, N_IMG)
    scale1 = 1.0 / math.sqrt(pixels)

    def fill_table(table, q, t):
        parts = depth // LANES
        for g in range(S // rows):
            start = coff_ref[q] + g * rows
            ll = iota((8, LANES), 1)
            jump = unit((start * LANES + 0 * ll) & (N_IMG - 1), N_IMG)
            jump = times((base[2], base[3]), (jump[0][0:1], jump[1][0:1]))
            here = slice(g * rows, (g + 1) * rows)
            if t == 0:
                along = unit((start * ll) & (N_IMG - 1), N_IMG)
                along = (along[0][0:1] * scale1, along[1][0:1] * scale1)
                now = times((base[0], base[1]), along)
            else:
                now = (state[0, here], state[1, here])
            for part in range(parts):
                lanes = slice(t * depth + part * LANES, t * depth + (part + 1) * LANES)
                table[g * rows : (g + 1) * rows, lanes] = now[0].astype(BF16)
                table[S + g * rows : S + (g + 1) * rows, lanes] = now[1].astype(BF16)
                now = times(now, jump)
            if t + 1 < chunks:
                state[0, here], state[1, here] = now

    def finish(band):
        band[0] = (prod[:S, :cols] + prod[S:, cols:]).astype(BF16)
        band[1] = (prod[:S, cols:] - prod[S:, :cols]).astype(BF16)

    first_y = f * pixels + chip * SCOL * cols
    wide = 2 * N_IMG
    drow = 2 * iota((half, LANES), 0) + 1
    scale2 = 1.0 / math.sqrt(pixels * n_f)

    def fill_second():
        y = first_y + iota((half, LANES), 1)
        now = unit(product(drow, y, wide), wide)
        now = (now[0] * scale2, now[1] * scale2)
        jump = unit((drow * LANES) & (wide - 1), wide)
        for part in range(SCOL * cols // LANES):
            lanes = slice(part * LANES, (part + 1) * LANES)
            table2[:half, lanes] = now[0].astype(BF16)
            table2[half:, lanes] = now[1].astype(BF16)
            now = times(now, jump)
        for i in range(per):
            y = first_y + iota((8, SCOL * cols), 1)
            offset = 2 * soff_ref[core * per + i] + S - 1
            shift_tab[0, i], shift_tab[1, i] = unit(product(offset, y, wide), wide)

    idx[: 2 * blocks] = cell_ref[...]
    idx[2 * blocks :] = frac_ref[...]

    def to_reader(step):
        rf, rp = step // n_p, lax.rem(step, n_p)
        target = rp * SCOL + side
        return (rf, rp, target), pltpu.make_async_remote_copy(
            src_ref=idx,
            dst_ref=idx_all.at[lax.rem(f, per), c],
            send_sem=isend_sem.at[rf, rp],
            recv_sem=irecv_sem.at[lax.rem(f, per), c],
            device_id={"facet": rf, "col": target},
        )

    def away(facet, col):
        return jnp.logical_or(facet != f, col != c)

    def send_index(step):
        step = lax.rem(step + f * n_p + chip, n_f * n_p)
        (rf, rp, target), copy = to_reader(step)

        @pl.when(away(rf, target))
        def _():
            copy.start()

    mine = core
    other = 1 - core
    tables = (table_a, table_b)
    fill_table(table_a, other, 0)
    fill_second()
    for t in range(chunks):
        if t + 1 < chunks:
            fill_table(table_a, other, t + 1)
        else:
            for u in range(chunks):
                fill_table(table_b, mine, u)
        here = slice(t * depth, (t + 1) * depth)
        for index in range(2):
            loads[2 * t + index].wait()
            at = slice(index * cols, (index + 1) * cols)
            term = jnp.dot(table_a[:, here], sky[index, here], preferred_element_type=F32)
            if t == 0:
                prod[:, at] = term
            else:
                prod[:, at] += term
        if t == 0:
            pl.semaphore_wait(barrier, everyone - 1)
            each(n_f * n_p, send_index)

            @pl.when(side == core)
            def _():
                idx_all[lax.rem(f, per), c] = idx[...]

    finish(bsend)
    swap = pltpu.make_async_remote_copy(
        src_ref=bsend,
        dst_ref=bands.at[core],
        send_sem=band_sem.at[0],
        recv_sem=band_sem.at[1],
        device_id={"facet": f, "col": chip * SCOL + other},
    )
    swap.start()

    def index_from(step):
        i, cc = step // n_c, lax.rem(step, n_c)

        @pl.when(away(core * per + i, cc))
        def _():
            pltpu.make_async_remote_copy(
                src_ref=idx,
                dst_ref=idx_all.at[i, cc],
                send_sem=isend_sem.at[0, 0],
                recv_sem=irecv_sem.at[i, cc],
                device_id={"facet": core * per + i, "col": cc},
            ).wait_recv()

    each(per * n_c, index_from)

    sub = iota((8, slots), 0)

    def prepare(step):
        i, cc = step // n_c, lax.rem(step, n_c)
        block = idx_all[i, cc]
        cell, frac = block[: 2 * blocks], block[2 * blocks :]
        match = [frac == row for row in range(over)]
        taps = []
        for tap in range(ksize):
            value = jnp.zeros(frac.shape, F32)
            for row in range(over):
                value = jnp.where(match[row], kern_ref[tap, row], value)
            taps.append(value)
        low, high = cell & 7, cell >> 3

        def window(b, line):
            lo = low[b : b + 1]
            turn = (line - lo) & 7
            value = jnp.zeros((8, slots), F32)
            for tap in range(ksize):
                value = jnp.where(turn == tap, taps[tap][b : b + 1], value)
            return value, high[b : b + 1] + jnp.where(line < lo, 1, 0)

        for b in range(blocks):
            row_r[i, cc, b], row_t[i, cc, b] = window(b, sub)
            col_r[i, cc, b, 0], col_t[i, cc, b, 0] = window(blocks + b, sub)
            col_r[i, cc, b, 1], col_t[i, cc, b, 1] = window(blocks + b, 7 - sub)

    for index in range(2):
        at = slice(index * cols, (index + 1) * cols)
        prod[:, at] = jnp.dot(table_b[...], sky[index], preferred_element_type=F32)
    each(per * n_c, prepare)
    finish(bands.at[core])
    swap.wait_recv()

    def grid_of(i):
        for h in range(SCOL):
            at = slice(h * cols, (h + 1) * cols)
            sc = shift_tab[0, i, 0:1, at]
            sd = shift_tab[1, i, 0:1, at]
            re = bands[h, 0].astype(F32)
            im = bands[h, 1].astype(F32)
            stacked[:S, at] = (re * sc + im * sd).astype(BF16)
            stacked[S:, at] = (im * sc - re * sd).astype(BF16)
        both = lax.dot_general(
            table2[...], stacked[...], (((1,), (1,)), ((), ())), preferred_element_type=F32
        )
        even_re, even_im = both[:half, :S], both[:half, S:]
        odd_re, odd_im = both[half:, :S], both[half:, S:]
        cells[:half] = (even_re + odd_im).astype(BF16)
        cells[half:S] = (even_re - odd_im).astype(BF16)
        cells[S : S + half] = (even_im - odd_re).astype(BF16)
        cells[S + half :] = (even_im + odd_re).astype(BF16)

    def vis_copy(i, cc):
        return pltpu.make_async_remote_copy(
            src_ref=vsend.at[i, cc],
            dst_ref=vrecv.at[f, chip],
            send_sem=vsend_sem.at[i, cc],
            recv_sem=vrecv_sem.at[f, chip],
            device_id={"facet": core * per + i, "col": cc},
        )

    def degrid(i, cc, slot):
        for b in range(blocks):
            lanes = slice(b * slots, (b + 1) * slots)
            value, at = row_r[i, cc, b], row_t[i, cc, b]
            for g in range(S // 16):
                pair = [jnp.where(at == 2 * g + k, value, 0.0) for k in range(2)]
                weights[slot, 16 * g : 16 * (g + 1), lanes] = jnp.concatenate(pair, axis=0).astype(BF16)
        summed = jnp.dot(cells[...], weights[slot], preferred_element_type=F32)
        for b in range(blocks):
            lanes = slice(b * slots, (b + 1) * slots)
            zero = jnp.zeros((8, slots), F32)
            total_re, total_im = zero, zero
            for k in range(2):
                value, at = col_r[i, cc, b, k], col_t[i, cc, b, k]
                acc_re, acc_im = zero, zero
                for g in range(half // 8):
                    hit = at == (half // 8 + g if k == 0 else half // 8 - 1 - g)
                    top = k * half + 8 * g
                    acc_re = jnp.where(hit, summed[top : top + 8, lanes], acc_re)
                    acc_im = jnp.where(hit, summed[S + top : S + top + 8, lanes], acc_im)
                total_re = total_re + value * acc_re
                total_im = total_im + value * acc_im
            vsend[i, cc, b : b + 1] = jnp.sum(total_re, axis=0, keepdims=True)
            vsend[i, cc, blocks + b : blocks + b + 1] = jnp.sum(total_im, axis=0, keepdims=True)

        @pl.when(away(core * per + i, cc))
        def _():
            vis_copy(i, cc).start()

        @pl.when(jnp.logical_not(away(core * per + i, cc)))
        def _():
            vrecv[f, chip] = vsend[i, cc]

    flip = jnp.where(f < core * per + per // 2, 1, 0)
    for step in range(per):
        i = step + flip * (per - 1 - 2 * step)
        grid_of(i)

        def to_owner(turn, i=i):
            cc = exclusive(c, n_c - 1 - turn, n_c)
            degrid(i, cc, turn % 2)

        each(n_c, to_owner)

    def vis_from(step):
        sf, sp = step // n_p, lax.rem(step, n_p)

        @pl.when(away(sf, sp * SCOL + side))
        def _():
            pltpu.make_async_remote_copy(
                src_ref=vrecv.at[sf, sp],
                dst_ref=vrecv.at[sf, sp],
                send_sem=vsend_sem.at[0, 0],
                recv_sem=vrecv_sem.at[sf, sp],
                device_id={"facet": sf, "col": sp * SCOL + side},
            ).wait_recv()

    each(n_f * n_p, vis_from)
    acc = jnp.zeros((2 * blocks, slots), F32)
    for sf in range(n_f):
        for sp in range(n_p):
            acc = acc + vrecv[sf, sp]
    for b in range(blocks):
        live = iota((1, slots), 1) < count_ref[b]
        vis_ref[b : b + 1] = jnp.where(live, acc[b : b + 1], 0.0)
        vis_ref[blocks + b : blocks + b + 1] = jnp.where(live, acc[blocks + b : blocks + b + 1], 0.0)

    swap.wait_send()

    def index_sent(step):
        (rf, rp, target), copy = to_reader(step)

        @pl.when(away(rf, target))
        def _():
            copy.wait_send()

    def vis_sent(step):
        i, cc = step // n_c, lax.rem(step, n_c)

        @pl.when(away(core * per + i, cc))
        def _():
            vis_copy(i, cc).wait_send()

    each(n_f * n_p, index_sent)
    each(per * n_c, vis_sent)


def local(sky_re, sky_im, col_offsets, sub_offsets, kernel, vis_count, cell_index, frac_index):
    n_f = lax.axis_size("facet")
    n_c = lax.axis_size("col")
    pixels, cols = sky_re.shape[1:]
    subs = sub_offsets.shape[0]
    owned, blocks = vis_count.shape
    slots = cell_index.shape[-1]
    over, ksize = kernel.shape
    assert owned == 1 and subs == n_f
    chunks = 4
    per = subs // SCOL
    n_p = n_c // SCOL
    dims = (n_f, n_c, pixels, cols, subs, blocks, slots, chunks, ksize, over)
    smem = pl.BlockSpec(memory_space=pltpu.SMEM)
    vmem = pl.BlockSpec(memory_space=pltpu.VMEM)
    anywhere = pl.BlockSpec(memory_space=pl.ANY)
    dma = pltpu.SemaphoreType.DMA
    vis = pl.pallas_call(
        functools.partial(body, dims),
        out_shape=jax.ShapeDtypeStruct((2 * blocks, slots), F32),
        in_specs=[smem, smem, smem, smem, vmem, vmem, anywhere, anywhere],
        out_specs=vmem,
        scratch_shapes=[
            pltpu.VMEM((2, pixels, cols), BF16),
            pltpu.VMEM((2 * S, pixels), BF16),
            pltpu.VMEM((2 * S, pixels), BF16),
            pltpu.VMEM((2, S, LANES), F32),
            pltpu.VMEM((2 * S, 2 * cols), F32),
            pltpu.VMEM((4, 64, LANES), F32),
            pltpu.VMEM((2, per, 8, SCOL * cols), F32),
            pltpu.VMEM((S, SCOL * cols), BF16),
            pltpu.VMEM((2 * S, SCOL * cols), BF16),
            pltpu.VMEM((SCOL, 2, S, cols), BF16),
            pltpu.VMEM((2, S, cols), BF16),
            pltpu.VMEM((2 * S, S), BF16),
            pltpu.VMEM((4 * blocks, slots), jnp.int32),
            pltpu.VMEM((per, n_c, 4 * blocks, slots), jnp.int32),
            pltpu.VMEM((per, n_c, blocks, 8, slots), F32),
            pltpu.VMEM((per, n_c, blocks, 8, slots), jnp.int32),
            pltpu.VMEM((per, n_c, blocks, 2, 8, slots), F32),
            pltpu.VMEM((per, n_c, blocks, 2, 8, slots), jnp.int32),
            pltpu.VMEM((2, S, blocks * slots), BF16),
            pltpu.VMEM((per, n_c, 2 * blocks, slots), F32),
            pltpu.VMEM((n_f, n_p, 2 * blocks, slots), F32),
            dma((chunks, 2)),
            dma((2,)),
            dma((n_f, n_p)),
            dma((per, n_c)),
            dma((per, n_c)),
            dma((n_f, n_p)),
        ],
        compiler_params=pltpu.CompilerParams(
            collective_id=0, has_side_effects=True, vmem_limit_bytes=60 << 20
        ),
    )(
        col_offsets,
        sub_offsets,
        kernel.T,
        vis_count.reshape(blocks),
        cell_index.reshape(2 * blocks, slots),
        frac_index.reshape(2 * blocks, slots),
        sky_re,
        sky_im,
    )
    vis = vis.reshape(2, 1, blocks, slots)
    return (vis[0], vis[1])


def solution(mesh):
    placed = (
        P("facet", None, "col"),
        P("facet", None, "col"),
        P(),
        P(),
        P(),
        P("facet", "col"),
        P(None, "facet", "col", None),
        P(None, "facet", "col", None),
    )
    return jax.shard_map(
        local,
        mesh=mesh,
        in_specs=placed,
        out_specs=(P("facet", "col", None), P("facet", "col", None)),
        check_vma=False,
    )
```

```python
import functools
import math

import jax
import jax.numpy as jnp
from jax import lax
from jax.experimental import pallas as pl
from jax.experimental.pallas import tpu as pltpu
from jax.sharding import PartitionSpec as P

N_IMG = 65536
S = 256
SCOL = 2
LANES = 128
F32 = jnp.float32
BF16 = jnp.bfloat16


def iota(shape, dim):
    return lax.broadcasted_iota(jnp.int32, shape, dim)


def unit(points, period):
    quarter = period // 4
    quad = (points + quarter // 2) >> (quarter.bit_length() - 1)
    x = (points - quad * quarter).astype(F32) * (2.0 * math.pi / period)
    x2 = x * x
    s = x2 * (1.0 / 362880) - 1.0 / 5040
    s = x2 * s + 1.0 / 120
    s = x2 * s - 1.0 / 6
    s = x * (x2 * s + 1.0)
    c = x2 * (1.0 / 40320) - 1.0 / 720
    c = x2 * c + 1.0 / 24
    c = x2 * c - 0.5
    c = x2 * c + 1.0
    odd = (quad & 1) != 0
    cos = jnp.where(odd, s, c)
    sin = jnp.where(odd, c, s)
    cos = jnp.where(((quad + 1) & 2) != 0, -cos, cos)
    sin = jnp.where((quad & 2) != 0, -sin, sin)
    return cos, sin


def product(left, right, period):
    upper = (left * (right >> 8)) & (period - 1)
    return (upper * 256 + left * (right & 255)) & (period - 1)


def times(left, right):
    return (
        left[0] * right[0] - left[1] * right[1],
        left[0] * right[1] + left[1] * right[0],
    )


def exclusive(left, right, count):
    total, bit = 0, 1
    while bit < count:
        total = total + ((left // bit) % 2 + (right // bit) % 2) % 2 * bit
        bit *= 2
    return total


def each(count, step):
    if count <= 16:
        for index in range(count):
            step(index)
    else:

        def once(index, carry):
            step(index)
            return carry

        lax.fori_loop(0, count, once, 0)


def body(
    dims,
    coff_ref,
    soff_ref,
    kern_ref,
    count_ref,
    cell_ref,
    frac_ref,
    re_hbm,
    im_hbm,
    vis_ref,
    sky,
    table_a,
    table_b,
    state,
    prod,
    base,
    shift_tab,
    table2,
    stacked,
    bands,
    bsend,
    cells,
    idx,
    idx_all,
    weights,
    vsend,
    vrecv,
    sky_sem,
    band_sem,
    isend_sem,
    irecv_sem,
    vsend_sem,
    vrecv_sem,
):
    n_f, n_c, pixels, cols, subs, blocks, slots, chunks, ksize, over = dims
    per = subs // SCOL
    n_p = n_c // SCOL
    rows = 64
    f = lax.axis_index("facet")
    c = lax.axis_index("col")
    core = lax.rem(c, SCOL)
    chip = c // SCOL
    side = f // per
    depth = pixels // chunks

    loads = []
    for t in range(chunks):
        for index, src in enumerate((re_hbm, im_hbm)):
            copy = pltpu.make_async_copy(
                src.at[0, pl.ds(t * depth, depth)],
                sky.at[index, pl.ds(t * depth, depth)],
                sky_sem.at[t, index],
            )
            copy.start()
            loads.append(copy)

    barrier = pltpu.get_barrier_semaphore()
    everyone = n_f * n_c

    def greet(step):
        other = lax.rem(f * n_c + c + 1 + step, everyone)
        pl.semaphore_signal(
            barrier, inc=1, device_id={"facet": other // n_c, "col": lax.rem(other, n_c)}
        )

    each(everyone - 1, greet)

    jrow = iota((rows, LANES), 0)
    lane = iota((rows, LANES), 1)
    base[0], base[1] = unit(jrow * lane, N_IMG)
    base[2], base[3] = unit(jrow * LANES, N_IMG)
    scale1 = 1.0 / math.sqrt(pixels)

    def fill_table(table, q, t):
        parts = depth // LANES
        for g in range(S // rows):
            start = coff_ref[q] + g * rows
            ll = iota((8, LANES), 1)
            jump = unit((start * LANES + 0 * ll) & (N_IMG - 1), N_IMG)
            jump = times((base[2], base[3]), (jump[0][0:1], jump[1][0:1]))
            here = slice(g * rows, (g + 1) * rows)
            if t == 0:
                along = unit((start * ll) & (N_IMG - 1), N_IMG)
                along = (along[0][0:1] * scale1, along[1][0:1] * scale1)
                now = times((base[0], base[1]), along)
            else:
                now = (state[0, here], state[1, here])
            for part in range(parts):
                lanes = slice(t * depth + part * LANES, t * depth + (part + 1) * LANES)
                table[g * rows : (g + 1) * rows, lanes] = now[0].astype(BF16)
                table[S + g * rows : S + (g + 1) * rows, lanes] = now[1].astype(BF16)
                now = times(now, jump)
            if t + 1 < chunks:
                state[0, here], state[1, here] = now

    def finish(band):
        band[0] = (prod[:S, :cols] + prod[S:, cols:]).astype(BF16)
        band[1] = (prod[:S, cols:] - prod[S:, :cols]).astype(BF16)

    first_y = f * pixels + chip * SCOL * cols
    scale2 = 1.0 / math.sqrt(pixels * n_f)

    def fill_second():
        for g in range(S // rows):
            k = iota((rows, LANES), 0) + g * rows
            y = first_y + iota((rows, LANES), 1)
            now = unit(product(k, y, N_IMG), N_IMG)
            now = (now[0] * scale2, now[1] * scale2)
            jump = unit((k * LANES) & (N_IMG - 1), N_IMG)
            for part in range(SCOL * cols // LANES):
                lanes = slice(part * LANES, (part + 1) * LANES)
                table2[g * rows : (g + 1) * rows, lanes] = now[0].astype(BF16)
                table2[S + g * rows : S + (g + 1) * rows, lanes] = now[1].astype(BF16)
                now = times(now, jump)
        for i in range(per):
            y = first_y + iota((8, SCOL * cols), 1)
            shift_tab[0, i], shift_tab[1, i] = unit(product(soff_ref[core * per + i], y, N_IMG), N_IMG)

    idx[: 2 * blocks] = cell_ref[...]
    idx[2 * blocks :] = frac_ref[...]

    def away(facet, col):
        return jnp.logical_or(facet != f, col != c)

    own_index = idx_all.at[lax.rem(f, per), c]
    own_sem = irecv_sem.at[lax.rem(f, per), c]

    def to_reader(step):
        rf = lax.rem(f + step // n_p, n_f)
        rp = lax.rem(chip + lax.rem(step, n_p), n_p)
        target = rp * SCOL + side
        return (rf, target), pltpu.make_async_remote_copy(
            src_ref=idx,
            dst_ref=own_index,
            send_sem=isend_sem.at[rf, rp],
            recv_sem=own_sem,
            device_id={"facet": rf, "col": target},
        )

    def send_index(step):
        (rf, target), copy = to_reader(step)
        if isinstance(step, int) and step > 0:
            copy.start()
            return

        @pl.when(away(rf, target))
        def _():
            copy.start()

        @pl.when(jnp.logical_not(away(rf, target)))
        def _():
            pltpu.make_async_copy(idx, own_index, own_sem).start()

    mine = core
    other = 1 - core
    tables = (table_a, table_b)
    fill_table(table_a, other, 0)
    fill_second()
    for t in range(chunks):
        if t + 1 < chunks:
            fill_table(table_a, other, t + 1)
        else:
            for u in range(chunks):
                fill_table(table_b, mine, u)
        here = slice(t * depth, (t + 1) * depth)
        for index in range(2):
            loads[2 * t + index].wait()
            at = slice(index * cols, (index + 1) * cols)
            term = jnp.dot(table_a[:, here], sky[index, here], preferred_element_type=F32)
            if t == 0:
                prod[:, at] = term
            else:
                prod[:, at] += term
    finish(bsend)
    swap = pltpu.make_async_remote_copy(
        src_ref=bsend,
        dst_ref=bands.at[core],
        send_sem=band_sem.at[0],
        recv_sem=band_sem.at[1],
        device_id={"facet": f, "col": chip * SCOL + other},
    )

    def index_from(i, cc):
        pltpu.make_async_copy(idx, idx_all.at[i, cc], irecv_sem.at[i, cc]).wait()

    sub = iota((8, slots), 0)

    sub16 = iota((16, slots), 0)

    def prepare(i, cc):
        block = idx_all[i, cc]
        cell, frac = block[: 2 * blocks], block[2 * blocks :]
        match = [frac == row for row in range(over)]
        taps = []
        for tap in range(ksize):
            value = jnp.zeros(frac.shape, F32)
            for row in range(over):
                value = jnp.where(match[row], kern_ref[tap, row], value)
            taps.append(value)

        def window(b, line):
            size = line.shape[0]
            lo = cell[b : b + 1] & (size - 1)
            turn = (line - lo) & (size - 1)
            value = jnp.zeros(line.shape, F32)
            for tap in range(ksize):
                value = jnp.where(turn == tap, taps[tap][b : b + 1], value)
            high = cell[b : b + 1] >> (size.bit_length() - 1)
            return value, high + jnp.where(line < lo, 1, 0)

        return [window(b, sub16) for b in range(blocks)], [window(blocks + b, sub) for b in range(blocks)]

    for index in range(2):
        at = slice(index * cols, (index + 1) * cols)
        prod[:, at] = jnp.dot(table_b[...], sky[index], preferred_element_type=F32)
        if index == 0:
            pl.semaphore_wait(barrier, everyone - 1)
            swap.start()
            each(n_f * n_p, send_index)
    finish(bands.at[core])
    swap.wait_recv()

    def grid_of(i):
        for h in range(SCOL):
            at = slice(h * cols, (h + 1) * cols)
            sc = shift_tab[0, i, 0:1, at]
            sd = shift_tab[1, i, 0:1, at]
            re = bands[h, 0].astype(F32)
            im = bands[h, 1].astype(F32)
            stacked[:S, at] = (re * sc + im * sd).astype(BF16)
            stacked[S:, at] = (im * sc - re * sd).astype(BF16)
        both = lax.dot_general(
            table2[...], stacked[...], (((1,), (1,)), ((), ())), preferred_element_type=F32
        )
        cells[i, :S] = (both[:S, :S] + both[S:, S:]).astype(BF16)
        cells[i, S:] = (both[:S, S:] - both[S:, :S]).astype(BF16)

    each(per, grid_of)

    def vis_copy(i, cc):
        return pltpu.make_async_remote_copy(
            src_ref=vsend.at[i, cc],
            dst_ref=vrecv.at[f, chip],
            send_sem=vsend_sem.at[i, cc],
            recv_sem=vrecv_sem.at[f, chip],
            device_id={"facet": core * per + i, "col": cc},
        )

    def degrid(i, cc, slot):
        row, col = prepare(i, cc)
        for b in range(blocks):
            lanes = slice(b * slots, (b + 1) * slots)
            value, at = row[b][0].astype(BF16), row[b][1].astype(jnp.int16)
            for g in range(S // 16):
                weights[slot, 16 * g : 16 * (g + 1), lanes] = jnp.where(
                    at == jnp.int16(g), value, jnp.zeros_like(value)
                )
        summed = jnp.dot(cells[i], weights[slot], preferred_element_type=F32)
        for b in range(blocks):
            lanes = slice(b * slots, (b + 1) * slots)
            value, at = col[b]
            acc_re = acc_im = jnp.zeros((8, slots), F32)
            for g in range(S // 8):
                hit = at == g
                acc_re = jnp.where(hit, summed[8 * g : 8 * g + 8, lanes], acc_re)
                acc_im = jnp.where(hit, summed[S + 8 * g : S + 8 * g + 8, lanes], acc_im)
            vsend[i, cc, b : b + 1] = jnp.sum(value * acc_re, axis=0, keepdims=True)
            vsend[i, cc, blocks + b : blocks + b + 1] = jnp.sum(value * acc_im, axis=0, keepdims=True)

    def send_vis(i, cc, near):
        if not near:
            vis_copy(i, cc).start()
            return

        @pl.when(away(core * per + i, cc))
        def _():
            vis_copy(i, cc).start()

        @pl.when(jnp.logical_not(away(core * per + i, cc)))
        def _():
            pltpu.make_async_copy(vsend.at[i, cc], vrecv.at[f, chip], vrecv_sem.at[f, chip]).start()

    flip = jnp.where(f < core * per + per // 2, 1, 0)
    batch = min(n_c, 4)
    for step in range(per):
        i = step + flip * (per - 1 - 2 * step)

        def arrive(cc, i=i):
            index_from(i, cc)

        each(n_c, arrive)

        def to_owners(turn, i=i):
            owners = [exclusive(c, n_c - 1 - turn * batch - k, n_c) for k in range(batch)]
            for k, cc in enumerate(owners):
                degrid(i, cc, k)
            for k, cc in enumerate(owners):
                last = k == batch - 1
                send_vis(i, cc, last if not isinstance(turn, int) else last and turn == n_c // batch - 1)

        each(n_c // batch, to_owners)

    def vis_from(step):
        sf, sp = step // n_p, lax.rem(step, n_p)
        pltpu.make_async_copy(vsend.at[0, 0], vrecv.at[sf, sp], vrecv_sem.at[sf, sp]).wait()

    each(n_f * n_p, vis_from)
    acc = jnp.zeros((2 * blocks, slots), F32)
    for sf in range(n_f):
        for sp in range(n_p):
            acc = acc + vrecv[sf, sp]
    for b in range(blocks):
        live = iota((1, slots), 1) < count_ref[b]
        vis_ref[b : b + 1] = jnp.where(live, acc[b : b + 1], 0.0)
        vis_ref[blocks + b : blocks + b + 1] = jnp.where(live, acc[blocks + b : blocks + b + 1], 0.0)

    swap.wait_send()

    def index_sent(step):
        (rf, target), copy = to_reader(step)
        if isinstance(step, int) and step > 0:
            copy.wait_send()
            return

        @pl.when(away(rf, target))
        def _():
            copy.wait_send()

    def vis_sent(step):
        i, cc = lax.rem(step, per), lax.rem(c + step // per, n_c)
        if isinstance(step, int) and step >= per:
            vis_copy(i, cc).wait_send()
            return

        @pl.when(away(core * per + i, cc))
        def _():
            vis_copy(i, cc).wait_send()

    each(n_f * n_p, index_sent)
    each(per * n_c, vis_sent)


def local(sky_re, sky_im, col_offsets, sub_offsets, kernel, vis_count, cell_index, frac_index):
    n_f = lax.axis_size("facet")
    n_c = lax.axis_size("col")
    pixels, cols = sky_re.shape[1:]
    subs = sub_offsets.shape[0]
    owned, blocks = vis_count.shape
    slots = cell_index.shape[-1]
    over, ksize = kernel.shape
    assert owned == 1 and subs == n_f
    chunks = 4
    per = subs // SCOL
    n_p = n_c // SCOL
    dims = (n_f, n_c, pixels, cols, subs, blocks, slots, chunks, ksize, over)
    smem = pl.BlockSpec(memory_space=pltpu.SMEM)
    vmem = pl.BlockSpec(memory_space=pltpu.VMEM)
    anywhere = pl.BlockSpec(memory_space=pl.ANY)
    dma = pltpu.SemaphoreType.DMA
    vis = pl.pallas_call(
        functools.partial(body, dims),
        out_shape=jax.ShapeDtypeStruct((2 * blocks, slots), F32),
        in_specs=[smem, smem, smem, smem, vmem, vmem, anywhere, anywhere],
        out_specs=vmem,
        scratch_shapes=[
            pltpu.VMEM((2, pixels, cols), BF16),
            pltpu.VMEM((2 * S, pixels), BF16),
            pltpu.VMEM((2 * S, pixels), BF16),
            pltpu.VMEM((2, S, LANES), F32),
            pltpu.VMEM((2 * S, 2 * cols), F32),
            pltpu.VMEM((4, 64, LANES), F32),
            pltpu.VMEM((2, per, 8, SCOL * cols), F32),
            pltpu.VMEM((2 * S, SCOL * cols), BF16),
            pltpu.VMEM((2 * S, SCOL * cols), BF16),
            pltpu.VMEM((SCOL, 2, S, cols), BF16),
            pltpu.VMEM((2, S, cols), BF16),
            pltpu.VMEM((per, 2 * S, S), BF16),
            pltpu.VMEM((4 * blocks, slots), jnp.int32),
            pltpu.VMEM((per, n_c, 4 * blocks, slots), jnp.int32),
            pltpu.VMEM((min(n_c, 4), S, blocks * slots), BF16),
            pltpu.VMEM((per, n_c, 2 * blocks, slots), F32),
            pltpu.VMEM((n_f, n_p, 2 * blocks, slots), F32),
            dma((chunks, 2)),
            dma((2,)),
            dma((n_f, n_p)),
            dma((per, n_c)),
            dma((per, n_c)),
            dma((n_f, n_p)),
        ],
        compiler_params=pltpu.CompilerParams(
            collective_id=0, has_side_effects=True, vmem_limit_bytes=60 << 20
        ),
    )(
        col_offsets,
        sub_offsets,
        kernel.T,
        vis_count.reshape(blocks),
        cell_index.reshape(2 * blocks, slots),
        frac_index.reshape(2 * blocks, slots),
        sky_re,
        sky_im,
    )
    vis = vis.reshape(2, 1, blocks, slots)
    return (vis[0], vis[1])


def solution(mesh):
    placed = (
        P("facet", None, "col"),
        P("facet", None, "col"),
        P(),
        P(),
        P(),
        P("facet", "col"),
        P(None, "facet", "col", None),
        P(None, "facet", "col", None),
    )
    return jax.shard_map(
        local,
        mesh=mesh,
        in_specs=placed,
        out_specs=(P("facet", "col", None), P("facet", "col", None)),
        check_vma=False,
    )
```

```python
import functools
import math

import jax
import jax.numpy as jnp
from jax import lax
from jax.experimental import pallas as pl
from jax.experimental.pallas import tpu as pltpu
from jax.sharding import PartitionSpec as P

N_IMG = 65536
S = 256
SCOL = 2
LANES = 128
F32 = jnp.float32
BF16 = jnp.bfloat16


def iota(shape, dim):
    return lax.broadcasted_iota(jnp.int32, shape, dim)


def unit(points, period):
    quarter = period // 4
    quad = (points + quarter // 2) >> (quarter.bit_length() - 1)
    x = (points - quad * quarter).astype(F32) * (2.0 * math.pi / period)
    x2 = x * x
    s = x2 * (1.0 / 362880) - 1.0 / 5040
    s = x2 * s + 1.0 / 120
    s = x2 * s - 1.0 / 6
    s = x * (x2 * s + 1.0)
    c = x2 * (1.0 / 40320) - 1.0 / 720
    c = x2 * c + 1.0 / 24
    c = x2 * c - 0.5
    c = x2 * c + 1.0
    odd = (quad & 1) != 0
    cos = jnp.where(odd, s, c)
    sin = jnp.where(odd, c, s)
    cos = jnp.where(((quad + 1) & 2) != 0, -cos, cos)
    sin = jnp.where((quad & 2) != 0, -sin, sin)
    return cos, sin


def product(left, right, period):
    upper = (left * (right >> 8)) & (period - 1)
    return (upper * 256 + left * (right & 255)) & (period - 1)


def times(left, right):
    return (
        left[0] * right[0] - left[1] * right[1],
        left[0] * right[1] + left[1] * right[0],
    )


def exclusive(left, right, count):
    total, bit = 0, 1
    while bit < count:
        total = total + ((left // bit) % 2 + (right // bit) % 2) % 2 * bit
        bit *= 2
    return total


def each(count, step):
    if count <= 16:
        for index in range(count):
            step(index)
    else:

        def once(index, carry):
            step(index)
            return carry

        lax.fori_loop(0, count, once, 0)


def body(
    dims,
    coff_ref,
    soff_ref,
    kern_ref,
    count_ref,
    cell_ref,
    frac_ref,
    re_hbm,
    im_hbm,
    vis_ref,
    sky,
    folded,
    table,
    flip_mat,
    state,
    prod,
    base,
    shift_tab,
    turn_tab,
    table2,
    stacked,
    bands,
    bsend,
    cells,
    idx,
    idx_all,
    weights,
    vsend,
    vrecv,
    sky_sem,
    band_sem,
    isend_sem,
    irecv_sem,
    vsend_sem,
    vrecv_sem,
):
    n_f, n_c, pixels, cols, subs, blocks, slots, chunks, ksize, over = dims
    per = subs // SCOL
    n_p = n_c // SCOL
    rows = 64
    f = lax.axis_index("facet")
    c = lax.axis_index("col")
    core = lax.rem(c, SCOL)
    chip = c // SCOL
    side = f // per
    depth = pixels // 2 // chunks
    wide = 2 * N_IMG

    loads = []
    for t in range(chunks):
        for k, start in enumerate((t * depth, pixels - (t + 1) * depth)):
            for index, src in enumerate((re_hbm, im_hbm)):
                copy = pltpu.make_async_copy(
                    src.at[0, pl.ds(start, depth)],
                    sky.at[index, pl.ds(start, depth)],
                    sky_sem.at[t, 2 * k + index],
                )
                copy.start()
                loads.append(copy)

    barrier = pltpu.get_barrier_semaphore()
    everyone = n_f * n_c

    def greet(step):
        other = lax.rem(f * n_c + c + 1 + step, everyone)
        pl.semaphore_signal(
            barrier, inc=1, device_id={"facet": other // n_c, "col": lax.rem(other, n_c)}
        )

    each(everyone - 1, greet)

    jrow = iota((rows, LANES), 0)
    twice = pixels - 1 - 2 * iota((rows, LANES), 1)
    base[0], base[1] = unit((jrow * twice) & (wide - 1), wide)
    base[2], base[3] = unit((jrow * (2 * LANES)) & (wide - 1), wide)
    scale1 = 1.0 / math.sqrt(pixels)
    order = (1 - core, core)

    def fill_table(t):
        for n, q in enumerate(order):
            for g in range(S // rows):
                start = coff_ref[q] + g * rows
                ll = pixels - 1 - 2 * iota((8, LANES), 1)
                jump = unit((start * (2 * LANES) + 0 * ll) & (wide - 1), wide)
                jump = times((base[2], base[3]), (jump[0][0:1], jump[1][0:1]))
                jump = (jump[0], -jump[1])
                here = slice(n * S + g * rows, n * S + (g + 1) * rows)
                if t == 0:
                    along = unit((start * ll) & (wide - 1), wide)
                    along = (along[0][0:1] * scale1, along[1][0:1] * scale1)
                    now = times((base[0], base[1]), along)
                else:
                    now = (state[0, here], state[1, here])
                for part in range(depth // LANES):
                    lanes = slice(2 * t * depth + part * LANES, 2 * t * depth + (part + 1) * LANES)
                    table[here, lanes] = now[0].astype(BF16)
                    lanes = slice(lanes.start + depth, lanes.stop + depth)
                    table[here, lanes] = now[1].astype(BF16)
                    now = times(now, jump)
                if t + 1 < chunks:
                    state[0, here], state[1, here] = now

    tile = flip_mat.shape[0]
    flip_mat[...] = jnp.where(iota((tile, tile), 0) + iota((tile, tile), 1) == tile - 1, 1.0, 0.0).astype(BF16)

    def fold(t):
        for index in range(2):
            loads[4 * t + index].wait()
            loads[4 * t + 2 + index].wait()
            here = slice(index * cols, (index + 1) * cols)
            there = slice((1 - index) * cols, (2 - index) * cols)
            for k in range(0, depth, tile):
                high = sky[index, pixels - t * depth - k - tile : pixels - t * depth - k]
                high = jnp.dot(flip_mat[...], high, preferred_element_type=F32).astype(BF16)
                low = sky[index, t * depth + k : t * depth + k + tile]
                top = 2 * t * depth + k
                folded[top : top + tile, here] = low + high
                top = top + depth
                folded[top : top + tile, there] = low - high if index == 0 else high - low

    def finish(band, top):
        for index in range(2):
            band[index] = prod[top : top + S, index * cols : (index + 1) * cols].astype(BF16)

    first_y = f * pixels + chip * SCOL * cols
    scale2 = 1.0 / math.sqrt(pixels * n_f)

    def fill_second():
        for g in range(S // rows):
            k = iota((rows, LANES), 0) + g * rows
            y = first_y + iota((rows, LANES), 1)
            now = unit(product(k, y, N_IMG), N_IMG)
            now = (now[0] * scale2, now[1] * scale2)
            jump = unit((k * LANES) & (N_IMG - 1), N_IMG)
            for part in range(SCOL * cols // LANES):
                lanes = slice(part * LANES, (part + 1) * LANES)
                table2[g * rows : (g + 1) * rows, lanes] = now[0].astype(BF16)
                table2[S + g * rows : S + (g + 1) * rows, lanes] = now[1].astype(BF16)
                now = times(now, jump)
        for i in range(per):
            y = first_y + iota((8, SCOL * cols), 1)
            shift_tab[0, i], shift_tab[1, i] = unit(product(soff_ref[core * per + i], y, N_IMG), N_IMG)

        j = coff_ref[core] + iota((8, S), 1)
        turn_tab[0], turn_tab[1] = unit((j * (pixels - 1)) & (wide - 1), wide)

    idx[: 2 * blocks] = cell_ref[...]
    idx[2 * blocks :] = frac_ref[...]

    def away(facet, col):
        return jnp.logical_or(facet != f, col != c)

    own_index = idx_all.at[lax.rem(f, per), c]
    own_sem = irecv_sem.at[lax.rem(f, per), c]

    def to_reader(step):
        rf = lax.rem(f + step // n_p, n_f)
        rp = lax.rem(chip + lax.rem(step, n_p), n_p)
        target = rp * SCOL + side
        return (rf, target), pltpu.make_async_remote_copy(
            src_ref=idx,
            dst_ref=own_index,
            send_sem=isend_sem.at[rf, rp],
            recv_sem=own_sem,
            device_id={"facet": rf, "col": target},
        )

    def send_index(step):
        (rf, target), copy = to_reader(step)
        if isinstance(step, int) and step > 0:
            copy.start()
            return

        @pl.when(away(rf, target))
        def _():
            copy.start()

        @pl.when(jnp.logical_not(away(rf, target)))
        def _():
            pltpu.make_async_copy(idx, own_index, own_sem).start()

    other = 1 - core
    fill_table(0)
    fold(0)
    fill_second()
    for t in range(chunks):
        if t + 1 < chunks:
            fill_table(t + 1)
            fold(t + 1)
        here = slice(2 * t * depth, 2 * (t + 1) * depth)
        for index in range(2):
            at = slice(index * cols, (index + 1) * cols)
            term = jnp.dot(table[:, here], folded[here, at], preferred_element_type=F32)
            if t == 0:
                prod[:, at] = term
            else:
                prod[:, at] += term

    finish(bsend, 0)
    swap = pltpu.make_async_remote_copy(
        src_ref=bsend,
        dst_ref=bands.at[core],
        send_sem=band_sem.at[0],
        recv_sem=band_sem.at[1],
        device_id={"facet": f, "col": chip * SCOL + other},
    )

    pl.semaphore_wait(barrier, everyone - 1)
    swap.start()
    each(n_f * n_p, send_index)

    def index_from(i, cc):
        pltpu.make_async_copy(idx, idx_all.at[i, cc], irecv_sem.at[i, cc]).wait()

    sub = iota((8, slots), 0)

    sub16 = iota((16, slots), 0)

    def prepare(i, cc):
        block = idx_all[i, cc]
        cell, frac = block[: 2 * blocks], block[2 * blocks :]
        match = [frac == row for row in range(over)]
        taps = []
        for tap in range(ksize):
            value = jnp.zeros(frac.shape, F32)
            for row in range(over):
                value = jnp.where(match[row], kern_ref[tap, row], value)
            taps.append(value)

        def window(b, line):
            size = line.shape[0]
            lo = cell[b : b + 1] & (size - 1)
            turn = (line - lo) & (size - 1)
            value = jnp.zeros(line.shape, F32)
            for tap in range(ksize):
                value = jnp.where(turn == tap, taps[tap][b : b + 1], value)
            high = cell[b : b + 1] >> (size.bit_length() - 1)
            return value, high + jnp.where(line < lo, 1, 0)

        return [window(b, sub16) for b in range(blocks)], [window(blocks + b, sub) for b in range(blocks)]

    finish(bands.at[core], S)
    swap.wait_recv()

    def grid_of(i):
        for h in range(SCOL):
            at = slice(h * cols, (h + 1) * cols)
            sc = shift_tab[0, i, 0:1, at]
            sd = shift_tab[1, i, 0:1, at]
            re = bands[h, 0].astype(F32)
            im = bands[h, 1].astype(F32)
            stacked[:S, at] = (re * sc + im * sd).astype(BF16)
            stacked[S:, at] = (im * sc - re * sd).astype(BF16)
        both = lax.dot_general(
            table2[...], stacked[...], (((1,), (1,)), ((), ())), preferred_element_type=F32
        )
        re = both[:S, :S] + both[S:, S:]
        im = both[:S, S:] - both[S:, :S]
        tc, td = turn_tab[0, 0:1], turn_tab[1, 0:1]
        cells[i, :S] = (re * tc + im * td).astype(BF16)
        cells[i, S:] = (im * tc - re * td).astype(BF16)

    each(per, grid_of)

    def vis_copy(i, cc):
        return pltpu.make_async_remote_copy(
            src_ref=vsend.at[i, cc],
            dst_ref=vrecv.at[f, chip],
            send_sem=vsend_sem.at[i, cc],
            recv_sem=vrecv_sem.at[f, chip],
            device_id={"facet": core * per + i, "col": cc},
        )

    def degrid(i, cc, slot):
        row, col = prepare(i, cc)
        for b in range(blocks):
            lanes = slice(b * slots, (b + 1) * slots)
            value, at = row[b][0].astype(BF16), row[b][1].astype(jnp.int16)
            for g in range(S // 16):
                weights[slot, 16 * g : 16 * (g + 1), lanes] = jnp.where(
                    at == jnp.int16(g), value, jnp.zeros_like(value)
                )
        summed = jnp.dot(cells[i], weights[slot], preferred_element_type=F32)
        for b in range(blocks):
            lanes = slice(b * slots, (b + 1) * slots)
            value, at = col[b]
            acc_re = acc_im = jnp.zeros((8, slots), F32)
            for g in range(S // 8):
                hit = at == g
                acc_re = jnp.where(hit, summed[8 * g : 8 * g + 8, lanes], acc_re)
                acc_im = jnp.where(hit, summed[S + 8 * g : S + 8 * g + 8, lanes], acc_im)
            vsend[i, cc, b : b + 1] = jnp.sum(value * acc_re, axis=0, keepdims=True)
            vsend[i, cc, blocks + b : blocks + b + 1] = jnp.sum(value * acc_im, axis=0, keepdims=True)

    def send_vis(i, cc, near):
        if not near:
            vis_copy(i, cc).start()
            return

        @pl.when(away(core * per + i, cc))
        def _():
            vis_copy(i, cc).start()

        @pl.when(jnp.logical_not(away(core * per + i, cc)))
        def _():
            pltpu.make_async_copy(vsend.at[i, cc], vrecv.at[f, chip], vrecv_sem.at[f, chip]).start()

    flip = jnp.where(f < core * per + per // 2, 1, 0)
    batch = min(n_c, 4)
    for step in range(per):
        i = step + flip * (per - 1 - 2 * step)

        def arrive(cc, i=i):
            index_from(i, cc)

        each(n_c, arrive)

        def to_owners(turn, i=i):
            owners = [exclusive(c, n_c - 1 - turn * batch - k, n_c) for k in range(batch)]
            for k, cc in enumerate(owners):
                degrid(i, cc, k)
            for k, cc in enumerate(owners):
                last = k == batch - 1
                send_vis(i, cc, last if not isinstance(turn, int) else last and turn == n_c // batch - 1)

        each(n_c // batch, to_owners)

    def vis_from(step):
        sf, sp = step // n_p, lax.rem(step, n_p)
        pltpu.make_async_copy(vsend.at[0, 0], vrecv.at[sf, sp], vrecv_sem.at[sf, sp]).wait()

    each(n_f * n_p, vis_from)
    acc = jnp.zeros((2 * blocks, slots), F32)
    for sf in range(n_f):
        for sp in range(n_p):
            acc = acc + vrecv[sf, sp]
    for b in range(blocks):
        live = iota((1, slots), 1) < count_ref[b]
        vis_ref[b : b + 1] = jnp.where(live, acc[b : b + 1], 0.0)
        vis_ref[blocks + b : blocks + b + 1] = jnp.where(live, acc[blocks + b : blocks + b + 1], 0.0)

    swap.wait_send()

    def index_sent(step):
        (rf, target), copy = to_reader(step)
        if isinstance(step, int) and step > 0:
            copy.wait_send()
            return

        @pl.when(away(rf, target))
        def _():
            copy.wait_send()

    def vis_sent(step):
        i, cc = lax.rem(step, per), lax.rem(c + step // per, n_c)
        if isinstance(step, int) and step >= per:
            vis_copy(i, cc).wait_send()
            return

        @pl.when(away(core * per + i, cc))
        def _():
            vis_copy(i, cc).wait_send()

    each(n_f * n_p, index_sent)
    each(per * n_c, vis_sent)


def local(sky_re, sky_im, col_offsets, sub_offsets, kernel, vis_count, cell_index, frac_index):
    n_f = lax.axis_size("facet")
    n_c = lax.axis_size("col")
    pixels, cols = sky_re.shape[1:]
    subs = sub_offsets.shape[0]
    owned, blocks = vis_count.shape
    slots = cell_index.shape[-1]
    over, ksize = kernel.shape
    assert owned == 1 and subs == n_f
    chunks = 4
    per = subs // SCOL
    n_p = n_c // SCOL
    dims = (n_f, n_c, pixels, cols, subs, blocks, slots, chunks, ksize, over)
    smem = pl.BlockSpec(memory_space=pltpu.SMEM)
    vmem = pl.BlockSpec(memory_space=pltpu.VMEM)
    anywhere = pl.BlockSpec(memory_space=pl.ANY)
    dma = pltpu.SemaphoreType.DMA
    vis = pl.pallas_call(
        functools.partial(body, dims),
        out_shape=jax.ShapeDtypeStruct((2 * blocks, slots), F32),
        in_specs=[smem, smem, smem, smem, vmem, vmem, anywhere, anywhere],
        out_specs=vmem,
        scratch_shapes=[
            pltpu.VMEM((2, pixels, cols), BF16),
            pltpu.VMEM((pixels, 2 * cols), BF16),
            pltpu.VMEM((2 * S, pixels), BF16),
            pltpu.VMEM((256, 256), BF16),
            pltpu.VMEM((2, 2 * S, LANES), F32),
            pltpu.VMEM((2 * S, 2 * cols), F32),
            pltpu.VMEM((4, 64, LANES), F32),
            pltpu.VMEM((2, per, 8, SCOL * cols), F32),
            pltpu.VMEM((2, 8, S), F32),
            pltpu.VMEM((2 * S, SCOL * cols), BF16),
            pltpu.VMEM((2 * S, SCOL * cols), BF16),
            pltpu.VMEM((SCOL, 2, S, cols), BF16),
            pltpu.VMEM((2, S, cols), BF16),
            pltpu.VMEM((per, 2 * S, S), BF16),
            pltpu.VMEM((4 * blocks, slots), jnp.int32),
            pltpu.VMEM((per, n_c, 4 * blocks, slots), jnp.int32),
            pltpu.VMEM((min(n_c, 4), S, blocks * slots), BF16),
            pltpu.VMEM((per, n_c, 2 * blocks, slots), F32),
            pltpu.VMEM((n_f, n_p, 2 * blocks, slots), F32),
            dma((chunks, 4)),
            dma((2,)),
            dma((n_f, n_p)),
            dma((per, n_c)),
            dma((per, n_c)),
            dma((n_f, n_p)),
        ],
        compiler_params=pltpu.CompilerParams(
            collective_id=0, has_side_effects=True, vmem_limit_bytes=60 << 20
        ),
    )(
        col_offsets,
        sub_offsets,
        kernel.T,
        vis_count.reshape(blocks),
        cell_index.reshape(2 * blocks, slots),
        frac_index.reshape(2 * blocks, slots),
        sky_re,
        sky_im,
    )
    vis = vis.reshape(2, 1, blocks, slots)
    return (vis[0], vis[1])


def solution(mesh):
    placed = (
        P("facet", None, "col"),
        P("facet", None, "col"),
        P(),
        P(),
        P(),
        P("facet", "col"),
        P(None, "facet", "col", None),
        P(None, "facet", "col", None),
    )
    return jax.shard_map(
        local,
        mesh=mesh,
        in_specs=placed,
        out_specs=(P("facet", "col", None), P("facet", "col", None)),
        check_vma=False,
    )
```

```python
import functools
import math

import jax
import jax.numpy as jnp
from jax import lax
from jax.experimental import pallas as pl
from jax.experimental.pallas import tpu as pltpu
from jax.sharding import PartitionSpec as P

N_IMG = 65536
S = 256
SCOL = 2
LANES = 128
F32 = jnp.float32
BF16 = jnp.bfloat16


def iota(shape, dim):
    return lax.broadcasted_iota(jnp.int32, shape, dim)


def unit(points, period):
    quarter = period // 4
    quad = (points + quarter // 2) >> (quarter.bit_length() - 1)
    x = (points - quad * quarter).astype(F32) * (2.0 * math.pi / period)
    x2 = x * x
    s = x2 * (1.0 / 362880) - 1.0 / 5040
    s = x2 * s + 1.0 / 120
    s = x2 * s - 1.0 / 6
    s = x * (x2 * s + 1.0)
    c = x2 * (1.0 / 40320) - 1.0 / 720
    c = x2 * c + 1.0 / 24
    c = x2 * c - 0.5
    c = x2 * c + 1.0
    odd = (quad & 1) != 0
    cos = jnp.where(odd, s, c)
    sin = jnp.where(odd, c, s)
    cos = jnp.where(((quad + 1) & 2) != 0, -cos, cos)
    sin = jnp.where((quad & 2) != 0, -sin, sin)
    return cos, sin


def product(left, right, period):
    upper = (left * (right >> 8)) & (period - 1)
    return (upper * 256 + left * (right & 255)) & (period - 1)


def times(left, right):
    return (
        left[0] * right[0] - left[1] * right[1],
        left[0] * right[1] + left[1] * right[0],
    )


def exclusive(left, right, count):
    total, bit = 0, 1
    while bit < count:
        total = total + ((left // bit) % 2 + (right // bit) % 2) % 2 * bit
        bit *= 2
    return total


def each(count, step):
    if count <= 16:
        for index in range(count):
            step(index)
    else:

        def once(index, carry):
            step(index)
            return carry

        lax.fori_loop(0, count, once, 0)


def body(
    dims,
    coff_ref,
    soff_ref,
    kern_ref,
    count_ref,
    cell_ref,
    frac_ref,
    re_hbm,
    im_hbm,
    vis_ref,
    sky,
    folded,
    table,
    flip_mat,
    state,
    prod,
    base,
    shift_tab,
    turn_tab,
    table2,
    stacked,
    bands,
    bsend,
    cells,
    idx,
    idx_all,
    weights,
    vsend,
    vrecv,
    sky_sem,
    band_sem,
    isend_sem,
    irecv_sem,
    vsend_sem,
    vrecv_sem,
):
    n_f, n_c, pixels, cols, subs, blocks, slots, chunks, ksize, over = dims
    per = subs // SCOL
    n_p = n_c // SCOL
    rows = 64
    f = lax.axis_index("facet")
    c = lax.axis_index("col")
    core = lax.rem(c, SCOL)
    chip = c // SCOL
    side = f // per
    depth = pixels // 2 // chunks
    wide = 2 * N_IMG

    loads = []
    for t in range(chunks):
        for k, start in enumerate((t * depth, pixels - (t + 1) * depth)):
            for index, src in enumerate((re_hbm, im_hbm)):
                copy = pltpu.make_async_copy(
                    src.at[0, pl.ds(start, depth)],
                    sky.at[index, pl.ds(start, depth)],
                    sky_sem.at[t, 2 * k + index],
                )
                copy.start()
                loads.append(copy)

    barrier = pltpu.get_barrier_semaphore()
    everyone = n_f * n_c

    def greet(step):
        other = lax.rem(f * n_c + c + 1 + step, everyone)
        pl.semaphore_signal(
            barrier, inc=1, device_id={"facet": other // n_c, "col": lax.rem(other, n_c)}
        )

    each(everyone - 1, greet)

    jrow = iota((rows, LANES), 0)
    twice = pixels - 1 - 2 * iota((rows, LANES), 1)
    base[0], base[1] = unit((jrow * twice) & (wide - 1), wide)
    base[2], base[3] = unit((jrow * (2 * LANES)) & (wide - 1), wide)
    scale1 = 1.0 / math.sqrt(pixels)
    order = (1 - core, core)

    def fill_table(t):
        for n, q in enumerate(order):
            for g in range(S // rows):
                start = coff_ref[q] + g * rows
                ll = pixels - 1 - 2 * iota((8, LANES), 1)
                jump = unit((start * (2 * LANES) + 0 * ll) & (wide - 1), wide)
                jump = times((base[2], base[3]), (jump[0][0:1], jump[1][0:1]))
                jump = (jump[0], -jump[1])
                here = slice(n * S + g * rows, n * S + (g + 1) * rows)
                if t == 0:
                    along = unit((start * ll) & (wide - 1), wide)
                    along = (along[0][0:1] * scale1, along[1][0:1] * scale1)
                    now = times((base[0], base[1]), along)
                else:
                    now = (state[0, here], state[1, here])
                for part in range(depth // LANES):
                    lanes = slice(2 * t * depth + part * LANES, 2 * t * depth + (part + 1) * LANES)
                    table[here, lanes] = now[0].astype(BF16)
                    lanes = slice(lanes.start + depth, lanes.stop + depth)
                    table[here, lanes] = now[1].astype(BF16)
                    now = times(now, jump)
                if t + 1 < chunks:
                    state[0, here], state[1, here] = now

    tile = flip_mat.shape[0]
    flip_mat[...] = jnp.where(iota((tile, tile), 0) + iota((tile, tile), 1) == tile - 1, 1.0, 0.0).astype(BF16)

    def fold(t):
        for index in range(2):
            here = slice(index * cols, (index + 1) * cols)
            there = slice((1 - index) * cols, (2 - index) * cols)
            for k in range(0, depth, tile):
                high = sky[index, pixels - t * depth - k - tile : pixels - t * depth - k]
                high = jnp.dot(flip_mat[...], high, preferred_element_type=F32).astype(BF16)
                low = sky[index, t * depth + k : t * depth + k + tile]
                top = 2 * t * depth + k
                folded[top : top + tile, here] = low + high
                top = top + depth
                folded[top : top + tile, there] = low - high if index == 0 else high - low

    def finish(band, top):
        for index in range(2):
            band[index] = prod[top : top + S, index * cols : (index + 1) * cols].astype(BF16)

    first_y = f * pixels + chip * SCOL * cols
    scale2 = 1.0 / math.sqrt(pixels * n_f)

    def fill_second():
        for h, place in enumerate((core, 1 - core)):
            begin = first_y + place * cols
            for g in range(S // rows):
                k = iota((rows, LANES), 0) + g * rows
                y = begin + iota((rows, LANES), 1)
                now = unit(product(k, y, N_IMG), N_IMG)
                now = (now[0] * scale2, now[1] * scale2)
                jump = unit((k * LANES) & (N_IMG - 1), N_IMG)
                for part in range(cols // LANES):
                    lanes = slice(h * cols + part * LANES, h * cols + (part + 1) * LANES)
                    table2[g * rows : (g + 1) * rows, lanes] = now[0].astype(BF16)
                    table2[S + g * rows : S + (g + 1) * rows, lanes] = now[1].astype(BF16)
                    now = times(now, jump)
            for i in range(per):
                at = slice(h * cols, (h + 1) * cols)
                y = begin + iota((8, cols), 1)
                turn = unit(product(soff_ref[core * per + i], y, N_IMG), N_IMG)
                shift_tab[0, i, :, at], shift_tab[1, i, :, at] = turn
        j = coff_ref[core] + iota((8, S), 1)
        turn_tab[0], turn_tab[1] = unit((j * (pixels - 1)) & (wide - 1), wide)

    both_index = jnp.concatenate([cell_ref[...], frac_ref[...]], axis=0)
    idx[...] = both_index.astype(F32).astype(BF16)

    def away(facet, col):
        return jnp.logical_or(facet != f, col != c)

    own_index = idx_all.at[lax.rem(f, per), c]
    own_sem = irecv_sem.at[lax.rem(f, per), c]

    def to_reader(step):
        rf = lax.rem(f + step // n_p, n_f)
        rp = lax.rem(chip + lax.rem(step, n_p), n_p)
        target = rp * SCOL + side
        return (rf, target), pltpu.make_async_remote_copy(
            src_ref=idx,
            dst_ref=own_index,
            send_sem=isend_sem.at[rf, rp],
            recv_sem=own_sem,
            device_id={"facet": rf, "col": target},
        )

    def send_index(step):
        (rf, target), copy = to_reader(step)
        if isinstance(step, int) and step > 0:
            copy.start()
            return

        @pl.when(away(rf, target))
        def _():
            copy.start()

        @pl.when(jnp.logical_not(away(rf, target)))
        def _():
            pltpu.make_async_copy(idx, own_index, own_sem).start()

    other = 1 - core
    def landed(t):
        for copy in loads[4 * t : 4 * t + 4]:
            copy.wait()

    fill_table(0)
    fill_second()
    landed(0)
    fold(0)
    fill_table(1)
    for t in range(chunks):
        if t + 1 < chunks:
            landed(t + 1)
            fold(t + 1)
        if 0 < t < chunks - 1:
            fill_table(t + 1)
        here = slice(2 * t * depth, 2 * (t + 1) * depth)
        for index in range(2):
            at = slice(index * cols, (index + 1) * cols)
            term = jnp.dot(table[:, here], folded[here, at], preferred_element_type=F32)
            if t == 0:
                prod[:, at] = term
            else:
                prod[:, at] += term
        if t == chunks // 2 - 1:
            pl.semaphore_wait(barrier, everyone - 1)
            each(n_f * n_p, send_index)

    finish(bsend, 0)
    swap = pltpu.make_async_remote_copy(
        src_ref=bsend,
        dst_ref=bands.at[1],
        send_sem=band_sem.at[0],
        recv_sem=band_sem.at[1],
        device_id={"facet": f, "col": chip * SCOL + other},
    )

    swap.start()

    def index_from(i, cc):
        pltpu.make_async_copy(idx, idx_all.at[i, cc], irecv_sem.at[i, cc]).wait()

    sub = iota((8, slots), 0)

    sub16 = iota((16, slots), 0)

    def prepare(i, cc):
        block = idx_all[i, cc].astype(F32).astype(jnp.int32)
        cell, frac = block[: 2 * blocks], block[2 * blocks :]
        match = [frac == row for row in range(over)]
        taps = []
        for tap in range(ksize):
            value = jnp.zeros(frac.shape, F32)
            for row in range(over):
                value = jnp.where(match[row], kern_ref[tap, row], value)
            taps.append(value)

        def window(b, line):
            size = line.shape[0]
            lo = cell[b : b + 1] & (size - 1)
            turn = (line - lo) & (size - 1)
            value = jnp.zeros(line.shape, F32)
            for tap in range(ksize):
                value = jnp.where(turn == tap, taps[tap][b : b + 1], value)
            high = cell[b : b + 1] >> (size.bit_length() - 1)
            return value, high + jnp.where(line < lo, 1, 0)

        return [window(b, sub16) for b in range(blocks)], [window(blocks + b, sub) for b in range(blocks)]

    finish(bands.at[0], S)

    def shift(h, step=16):
        for part in range(cols // LANES):
            near = slice(part * LANES, (part + 1) * LANES)
            at = slice(h * cols + near.start, h * cols + near.stop)
            for top in range(0, S, step):
                re = bands[h, 0, top : top + step, near].astype(F32)
                im = bands[h, 1, top : top + step, near].astype(F32)
                for i in range(per):
                    sc = shift_tab[0, i, 0:1, at]
                    sd = shift_tab[1, i, 0:1, at]
                    stacked[i, top : top + step, at] = (re * sc + im * sd).astype(BF16)
                    stacked[i, S + top : S + top + step, at] = (im * sc - re * sd).astype(BF16)

    shift(0)
    swap.wait_recv()
    shift(1)

    def grid_of(i):
        both = lax.dot_general(
            table2[...], stacked[i], (((1,), (1,)), ((), ())), preferred_element_type=F32
        )
        re = both[:S, :S] + both[S:, S:]
        im = both[:S, S:] - both[S:, :S]
        tc, td = turn_tab[0, 0:1], turn_tab[1, 0:1]
        cells[i, :S] = (re * tc + im * td).astype(BF16)
        cells[i, S:] = (im * tc - re * td).astype(BF16)

    each(per, grid_of)

    def vis_copy(i, cc):
        return pltpu.make_async_remote_copy(
            src_ref=vsend.at[i, cc],
            dst_ref=vrecv.at[f, chip],
            send_sem=vsend_sem.at[i, cc],
            recv_sem=vrecv_sem.at[f, chip],
            device_id={"facet": core * per + i, "col": cc},
        )

    def degrid(i, cc, slot):
        row, col = prepare(i, cc)
        for b in range(blocks):
            lanes = slice(b * slots, (b + 1) * slots)
            value, at = row[b][0].astype(BF16), row[b][1].astype(jnp.int16)
            for g in range(S // 16):
                weights[slot, 16 * g : 16 * (g + 1), lanes] = jnp.where(
                    at == jnp.int16(g), value, jnp.zeros_like(value)
                )
        summed = jnp.dot(cells[i], weights[slot], preferred_element_type=F32)
        for b in range(blocks):
            lanes = slice(b * slots, (b + 1) * slots)
            value, at = col[b]
            acc_re = acc_im = jnp.zeros((8, slots), F32)
            for g in range(S // 8):
                hit = at == g
                acc_re = jnp.where(hit, summed[8 * g : 8 * g + 8, lanes], acc_re)
                acc_im = jnp.where(hit, summed[S + 8 * g : S + 8 * g + 8, lanes], acc_im)
            vsend[i, cc, b : b + 1] = jnp.sum(value * acc_re, axis=0, keepdims=True)
            vsend[i, cc, blocks + b : blocks + b + 1] = jnp.sum(value * acc_im, axis=0, keepdims=True)

    def send_vis(i, cc, near):
        if not near:
            vis_copy(i, cc).start()
            return

        @pl.when(away(core * per + i, cc))
        def _():
            vis_copy(i, cc).start()

        @pl.when(jnp.logical_not(away(core * per + i, cc)))
        def _():
            pltpu.make_async_copy(vsend.at[i, cc], vrecv.at[f, chip], vrecv_sem.at[f, chip]).start()

    flip = jnp.where(f < core * per + per // 2, 1, 0)
    batch = min(n_c, 4)
    for step in range(per):
        i = step + flip * (per - 1 - 2 * step)

        def arrive(cc, i=i):
            index_from(i, cc)

        each(n_c, arrive)

        def to_owners(turn, i=i):
            owners = [exclusive(c, n_c - 1 - turn * batch - k, n_c) for k in range(batch)]
            for k, cc in enumerate(owners):
                degrid(i, cc, k)
            for k, cc in enumerate(owners):
                last = k == batch - 1
                send_vis(i, cc, last if not isinstance(turn, int) else last and turn == n_c // batch - 1)

        each(n_c // batch, to_owners)

    def vis_from(step):
        sf, sp = step // n_p, lax.rem(step, n_p)
        pltpu.make_async_copy(vsend.at[0, 0], vrecv.at[sf, sp], vrecv_sem.at[sf, sp]).wait()

    each(n_f * n_p, vis_from)
    acc = jnp.zeros((2 * blocks, slots), F32)
    for sf in range(n_f):
        for sp in range(n_p):
            acc = acc + vrecv[sf, sp]
    for b in range(blocks):
        live = iota((1, slots), 1) < count_ref[b]
        vis_ref[b : b + 1] = jnp.where(live, acc[b : b + 1], 0.0)
        vis_ref[blocks + b : blocks + b + 1] = jnp.where(live, acc[blocks + b : blocks + b + 1], 0.0)

    swap.wait_send()

    def index_sent(step):
        (rf, target), copy = to_reader(step)
        if isinstance(step, int) and step > 0:
            copy.wait_send()
            return

        @pl.when(away(rf, target))
        def _():
            copy.wait_send()

    def vis_sent(step):
        i, cc = lax.rem(step, per), lax.rem(c + step // per, n_c)
        if isinstance(step, int) and step >= per:
            vis_copy(i, cc).wait_send()
            return

        @pl.when(away(core * per + i, cc))
        def _():
            vis_copy(i, cc).wait_send()

    each(n_f * n_p, index_sent)
    each(per * n_c, vis_sent)


def local(sky_re, sky_im, col_offsets, sub_offsets, kernel, vis_count, cell_index, frac_index):
    n_f = lax.axis_size("facet")
    n_c = lax.axis_size("col")
    pixels, cols = sky_re.shape[1:]
    subs = sub_offsets.shape[0]
    owned, blocks = vis_count.shape
    slots = cell_index.shape[-1]
    over, ksize = kernel.shape
    assert owned == 1 and subs == n_f
    chunks = 4
    per = subs // SCOL
    n_p = n_c // SCOL
    dims = (n_f, n_c, pixels, cols, subs, blocks, slots, chunks, ksize, over)
    smem = pl.BlockSpec(memory_space=pltpu.SMEM)
    vmem = pl.BlockSpec(memory_space=pltpu.VMEM)
    anywhere = pl.BlockSpec(memory_space=pl.ANY)
    dma = pltpu.SemaphoreType.DMA
    vis = pl.pallas_call(
        functools.partial(body, dims),
        out_shape=jax.ShapeDtypeStruct((2 * blocks, slots), F32),
        in_specs=[smem, smem, smem, smem, vmem, vmem, anywhere, anywhere],
        out_specs=vmem,
        scratch_shapes=[
            pltpu.VMEM((2, pixels, cols), BF16),
            pltpu.VMEM((pixels, 2 * cols), BF16),
            pltpu.VMEM((2 * S, pixels), BF16),
            pltpu.VMEM((256, 256), BF16),
            pltpu.VMEM((2, 2 * S, LANES), F32),
            pltpu.VMEM((2 * S, 2 * cols), F32),
            pltpu.VMEM((4, 64, LANES), F32),
            pltpu.VMEM((2, per, 8, SCOL * cols), F32),
            pltpu.VMEM((2, 8, S), F32),
            pltpu.VMEM((2 * S, SCOL * cols), BF16),
            pltpu.VMEM((per, 2 * S, SCOL * cols), BF16),
            pltpu.VMEM((SCOL, 2, S, cols), BF16),
            pltpu.VMEM((2, S, cols), BF16),
            pltpu.VMEM((per, 2 * S, S), BF16),
            pltpu.VMEM((4 * blocks, slots), BF16),
            pltpu.VMEM((per, n_c, 4 * blocks, slots), BF16),
            pltpu.VMEM((min(n_c, 4), S, blocks * slots), BF16),
            pltpu.VMEM((per, n_c, 2 * blocks, slots), F32),
            pltpu.VMEM((n_f, n_p, 2 * blocks, slots), F32),
            dma((chunks, 4)),
            dma((2,)),
            dma((n_f, n_p)),
            dma((per, n_c)),
            dma((per, n_c)),
            dma((n_f, n_p)),
        ],
        compiler_params=pltpu.CompilerParams(
            collective_id=0, has_side_effects=True, vmem_limit_bytes=60 << 20
        ),
    )(
        col_offsets,
        sub_offsets,
        kernel.T,
        vis_count.reshape(blocks),
        cell_index.reshape(2 * blocks, slots),
        frac_index.reshape(2 * blocks, slots),
        sky_re,
        sky_im,
    )
    vis = vis.reshape(2, 1, blocks, slots)
    return (vis[0], vis[1])


def solution(mesh):
    placed = (
        P("facet", None, "col"),
        P("facet", None, "col"),
        P(),
        P(),
        P(),
        P("facet", "col"),
        P(None, "facet", "col", None),
        P(None, "facet", "col", None),
    )
    return jax.shard_map(
        local,
        mesh=mesh,
        in_specs=placed,
        out_specs=(P("facet", "col", None), P("facet", "col", None)),
        check_vma=False,
    )
```

```python
import functools
import math

import jax
import jax.numpy as jnp
from jax import lax
from jax.experimental import pallas as pl
from jax.experimental.pallas import tpu as pltpu
from jax.sharding import PartitionSpec as P

N_IMG = 65536
S = 256
SCOL = 2
LANES = 128
F32 = jnp.float32
BF16 = jnp.bfloat16


def iota(shape, dim):
    return lax.broadcasted_iota(jnp.int32, shape, dim)


def unit(points, period):
    quarter = period // 4
    quad = (points + quarter // 2) >> (quarter.bit_length() - 1)
    x = (points - quad * quarter).astype(F32) * (2.0 * math.pi / period)
    x2 = x * x
    s = x2 * (1.0 / 362880) - 1.0 / 5040
    s = x2 * s + 1.0 / 120
    s = x2 * s - 1.0 / 6
    s = x * (x2 * s + 1.0)
    c = x2 * (1.0 / 40320) - 1.0 / 720
    c = x2 * c + 1.0 / 24
    c = x2 * c - 0.5
    c = x2 * c + 1.0
    odd = (quad & 1) != 0
    cos = jnp.where(odd, s, c)
    sin = jnp.where(odd, c, s)
    cos = jnp.where(((quad + 1) & 2) != 0, -cos, cos)
    sin = jnp.where((quad & 2) != 0, -sin, sin)
    return cos, sin


def product(left, right, period):
    upper = (left * (right >> 8)) & (period - 1)
    return (upper * 256 + left * (right & 255)) & (period - 1)


def times(left, right):
    return (
        left[0] * right[0] - left[1] * right[1],
        left[0] * right[1] + left[1] * right[0],
    )


def exclusive(left, right, count):
    total, bit = 0, 1
    while bit < count:
        total = total + ((left // bit) % 2 + (right // bit) % 2) % 2 * bit
        bit *= 2
    return total


def each(count, step):
    if count <= 16:
        for index in range(count):
            step(index)
    else:

        def once(index, carry):
            step(index)
            return carry

        lax.fori_loop(0, count, once, 0)


def body(
    dims,
    coff_ref,
    soff_ref,
    kern_ref,
    count_ref,
    cell_ref,
    frac_ref,
    re_hbm,
    im_hbm,
    vis_ref,
    sky,
    folded,
    table,
    flip_mat,
    state,
    jumps,
    prod,
    base,
    shift_tab,
    turn_tab,
    table2,
    stacked,
    bands,
    bsend,
    cells,
    idx,
    idx_all,
    kern_vec,
    tap_buf,
    cell_buf,
    row_buf,
    at_buf,
    weights,
    vsend,
    vrecv,
    sky_sem,
    band_sem,
    isend_sem,
    irecv_sem,
    vsend_sem,
    vrecv_sem,
):
    n_f, n_c, pixels, cols, subs, blocks, slots, chunks, ksize, over = dims
    per = subs // SCOL
    n_p = n_c // SCOL
    rows = 64
    f = lax.axis_index("facet")
    c = lax.axis_index("col")
    core = lax.rem(c, SCOL)
    chip = c // SCOL
    side = f // per
    depth = pixels // 2 // chunks
    wide = 2 * N_IMG

    loads = []
    for t in range(chunks):
        for k, start in enumerate((t * depth, pixels - (t + 1) * depth)):
            for index, src in enumerate((re_hbm, im_hbm)):
                copy = pltpu.make_async_copy(
                    src.at[0, pl.ds(start, depth)],
                    sky.at[index, pl.ds(start, depth)],
                    sky_sem.at[t, 2 * k + index],
                )
                copy.start()
                loads.append(copy)

    barrier = pltpu.get_barrier_semaphore()
    everyone = n_f * n_c

    def greet(step):
        other = lax.rem(f * n_c + c + 1 + step, everyone)
        pl.semaphore_signal(
            barrier, inc=1, device_id={"facet": other // n_c, "col": lax.rem(other, n_c)}
        )

    each(everyone - 1, greet)

    jrow = iota((rows, LANES), 0)
    twice = pixels - 1 - 2 * iota((rows, LANES), 1)
    base[0], base[1] = unit((jrow * twice) & (wide - 1), wide)
    base[2], base[3] = unit((jrow * (2 * LANES)) & (wide - 1), wide)
    scale1 = 1.0 / math.sqrt(pixels)
    order = (1 - core, core)

    def fill_table(t):
        for n, q in enumerate(order):
            for g in range(S // rows):
                start = coff_ref[q] + g * rows
                here = slice(n * S + g * rows, n * S + (g + 1) * rows)
                if t == 0:
                    ll = pixels - 1 - 2 * iota((8, LANES), 1)
                    jump = unit((start * (2 * LANES) + 0 * ll) & (wide - 1), wide)
                    jump = times((base[2], base[3]), (jump[0][0:1], jump[1][0:1]))
                    jump = (jump[0], -jump[1])
                    jumps[0, here], jumps[1, here] = jump
                    along = unit((start * ll) & (wide - 1), wide)
                    along = (along[0][0:1] * scale1, along[1][0:1] * scale1)
                    now = times((base[0], base[1]), along)
                else:
                    jump = (jumps[0, here], jumps[1, here])
                    now = (state[0, here], state[1, here])
                for part in range(depth // LANES):
                    lanes = slice(2 * t * depth + part * LANES, 2 * t * depth + (part + 1) * LANES)
                    table[here, lanes] = now[0].astype(BF16)
                    lanes = slice(lanes.start + depth, lanes.stop + depth)
                    table[here, lanes] = now[1].astype(BF16)
                    now = times(now, jump)
                if t + 1 < chunks:
                    state[0, here], state[1, here] = now

    tile = flip_mat.shape[0]
    flip_mat[...] = jnp.where(iota((tile, tile), 0) + iota((tile, tile), 1) == tile - 1, 1.0, 0.0).astype(BF16)

    def fold(t):
        for index in range(2):
            here = slice(index * cols, (index + 1) * cols)
            there = slice((1 - index) * cols, (2 - index) * cols)
            for k in range(0, depth, tile):
                high = sky[index, pixels - t * depth - k - tile : pixels - t * depth - k]
                high = jnp.dot(flip_mat[...], high, preferred_element_type=F32).astype(BF16)
                low = sky[index, t * depth + k : t * depth + k + tile]
                top = 2 * t * depth + k
                folded[top : top + tile, here] = low + high
                top = top + depth
                folded[top : top + tile, there] = low - high if index == 0 else high - low

    def finish(band, top):
        for index in range(2):
            band[index] = prod[top : top + S, index * cols : (index + 1) * cols].astype(BF16)

    first_y = f * pixels + chip * SCOL * cols
    scale2 = 1.0 / math.sqrt(pixels * n_f)

    def fill_second():
        for h, place in enumerate((core, 1 - core)):
            begin = first_y + place * cols
            for g in range(S // rows):
                k = iota((rows, LANES), 0) + g * rows
                y = begin + iota((rows, LANES), 1)
                now = unit(product(k, y, N_IMG), N_IMG)
                now = (now[0] * scale2, now[1] * scale2)
                jump = unit((k * LANES) & (N_IMG - 1), N_IMG)
                for part in range(cols // LANES):
                    lanes = slice(h * cols + part * LANES, h * cols + (part + 1) * LANES)
                    table2[g * rows : (g + 1) * rows, lanes] = now[0].astype(BF16)
                    table2[S + g * rows : S + (g + 1) * rows, lanes] = now[1].astype(BF16)
                    now = times(now, jump)
            for i in range(per):
                at = slice(h * cols, (h + 1) * cols)
                y = begin + iota((8, cols), 1)
                turn = unit(product(soff_ref[core * per + i], y, N_IMG), N_IMG)
                shift_tab[0, i, :, at], shift_tab[1, i, :, at] = turn
        j = coff_ref[core] + iota((8, S), 1)
        turn_tab[0], turn_tab[1] = unit((j * (pixels - 1)) & (wide - 1), wide)

    both_index = jnp.concatenate([cell_ref[...], frac_ref[...]], axis=0)
    idx[...] = both_index.astype(F32).astype(BF16)

    def away(facet, col):
        return jnp.logical_or(facet != f, col != c)

    own_index = idx_all.at[lax.rem(f, per), c]
    own_sem = irecv_sem.at[lax.rem(f, per), c]

    def to_reader(step):
        rf = lax.rem(f + step // n_p, n_f)
        rp = lax.rem(chip + lax.rem(step, n_p), n_p)
        target = rp * SCOL + side
        return (rf, target), pltpu.make_async_remote_copy(
            src_ref=idx,
            dst_ref=own_index,
            send_sem=isend_sem.at[rf, rp],
            recv_sem=own_sem,
            device_id={"facet": rf, "col": target},
        )

    def send_index(step):
        (rf, target), copy = to_reader(step)
        if isinstance(step, int) and step > 0:
            copy.start()
            return

        @pl.when(away(rf, target))
        def _():
            copy.start()

        @pl.when(jnp.logical_not(away(rf, target)))
        def _():
            pltpu.make_async_copy(idx, own_index, own_sem).start()

    other = 1 - core
    def landed(t):
        for copy in loads[4 * t : 4 * t + 4]:
            copy.wait()

    for tap in range(ksize):
        for step in range(over):
            kern_vec[tap, step] = jnp.full((2 * blocks, slots), kern_ref[tap, step], F32)

    split = chunks // 2
    fill_table(0)
    fill_second()
    landed(0)
    fold(0)
    fill_table(1)
    for t in range(chunks):
        if t + 1 < chunks:
            landed(t + 1)
            fold(t + 1)
        if 0 < t < chunks - 1:
            fill_table(t + 1)
        here = slice(2 * t * depth, 2 * (t + 1) * depth)
        lines = slice(0, S if t >= split else 2 * S)
        for index in range(2):
            at = slice(index * cols, (index + 1) * cols)
            term = jnp.dot(table[lines, here], folded[here, at], preferred_element_type=F32)
            if t == 0:
                prod[lines, at] = term
            else:
                prod[lines, at] += term
        if t == chunks // 2 - 1:
            pl.semaphore_wait(barrier, everyone - 1)
            each(n_f * n_p, send_index)

    finish(bsend, 0)
    swap = pltpu.make_async_remote_copy(
        src_ref=bsend,
        dst_ref=bands.at[1],
        send_sem=band_sem.at[0],
        recv_sem=band_sem.at[1],
        device_id={"facet": f, "col": chip * SCOL + other},
    )

    swap.start()

    def index_from(i, cc):
        pltpu.make_async_copy(idx, idx_all.at[i, cc], irecv_sem.at[i, cc]).wait()

    sub = iota((8, slots), 0)

    sub16 = iota((16, slots), 0)

    def prepare(i, cc, slot):
        block = idx_all[i, cc].astype(F32).astype(jnp.int32)
        frac = block[2 * blocks :]
        cell_buf[slot] = block[: 2 * blocks]
        for tap in range(ksize):
            values = [kern_vec[tap, step] for step in range(over)]
            bit = 1
            while len(values) > 1:
                odd = (frac & bit) != 0
                values = [jnp.where(odd, high, low) for low, high in zip(values[::2], values[1::2])]
                bit *= 2
            tap_buf[slot, tap] = values[0]

        def window(b, line):
            size = line.shape[0]
            cell = jnp.broadcast_to(cell_buf[slot, b : b + 1], line.shape)
            lo = cell & (size - 1)
            turn = (line - lo) & (size - 1)
            value = jnp.zeros(line.shape, F32)
            for tap in range(ksize):
                value = jnp.where(turn == tap, tap_buf[slot, tap, b : b + 1], value)
            high = cell >> (size.bit_length() - 1)
            return value, high + jnp.where(line < lo, 1, 0)

        for b in range(blocks):
            value, at = window(b, sub16)
            row_buf[slot, b] = value.astype(BF16)
            at_buf[slot, b] = at.astype(jnp.int16)
        return [window(blocks + b, sub) for b in range(blocks)]

    here = slice(2 * split * depth, pixels)
    for index in range(2):
        at = slice(index * cols, (index + 1) * cols)
        prod[S:, at] += jnp.dot(table[S:, here], folded[here, at], preferred_element_type=F32)
    finish(bands.at[0], S)

    def shift(h, step=16):
        for part in range(cols // LANES):
            near = slice(part * LANES, (part + 1) * LANES)
            at = slice(h * cols + near.start, h * cols + near.stop)
            for top in range(0, S, step):
                re = bands[h, 0, top : top + step, near].astype(F32)
                im = bands[h, 1, top : top + step, near].astype(F32)
                for i in range(per):
                    sc = shift_tab[0, i, 0:1, at]
                    sd = shift_tab[1, i, 0:1, at]
                    stacked[i, top : top + step, at] = (re * sc + im * sd).astype(BF16)
                    stacked[i, S + top : S + top + step, at] = (im * sc - re * sd).astype(BF16)

    shift(0)
    swap.wait_recv()
    shift(1)

    def grid_of(i):
        both = lax.dot_general(
            table2[...], stacked[i], (((1,), (1,)), ((), ())), preferred_element_type=F32
        )
        re = both[:S, :S] + both[S:, S:]
        im = both[:S, S:] - both[S:, :S]
        tc, td = turn_tab[0, 0:1], turn_tab[1, 0:1]
        cells[i, :S] = (re * tc + im * td).astype(BF16)
        cells[i, S:] = (im * tc - re * td).astype(BF16)

    each(per, grid_of)

    def vis_copy(i, cc):
        return pltpu.make_async_remote_copy(
            src_ref=vsend.at[i, cc],
            dst_ref=vrecv.at[f, chip],
            send_sem=vsend_sem.at[i, cc],
            recv_sem=vrecv_sem.at[f, chip],
            device_id={"facet": core * per + i, "col": cc},
        )

    def degrid(i, cc, slot):
        col = prepare(i, cc, slot)
        for b in range(blocks):
            lanes = slice(b * slots, (b + 1) * slots)
            value, at = row_buf[slot, b], at_buf[slot, b]
            for g in range(S // 16):
                weights[slot, 16 * g : 16 * (g + 1), lanes] = jnp.where(
                    at == jnp.int16(g), value, jnp.zeros_like(value)
                )
        summed = jnp.dot(cells[i], weights[slot], preferred_element_type=F32)
        for b in range(blocks):
            lanes = slice(b * slots, (b + 1) * slots)
            value, at = col[b]
            acc_re = acc_im = jnp.zeros((8, slots), F32)
            for g in range(S // 8):
                hit = at == g
                acc_re = jnp.where(hit, summed[8 * g : 8 * g + 8, lanes], acc_re)
                acc_im = jnp.where(hit, summed[S + 8 * g : S + 8 * g + 8, lanes], acc_im)
            vsend[i, cc, b : b + 1] = jnp.sum(value * acc_re, axis=0, keepdims=True)
            vsend[i, cc, blocks + b : blocks + b + 1] = jnp.sum(value * acc_im, axis=0, keepdims=True)

    def send_vis(i, cc, near):
        if not near:
            vis_copy(i, cc).start()
            return

        @pl.when(away(core * per + i, cc))
        def _():
            vis_copy(i, cc).start()

        @pl.when(jnp.logical_not(away(core * per + i, cc)))
        def _():
            pltpu.make_async_copy(vsend.at[i, cc], vrecv.at[f, chip], vrecv_sem.at[f, chip]).start()

    flip = jnp.where(f < core * per + per // 2, 1, 0)
    batch = min(n_c, 4)
    for step in range(per):
        i = step + flip * (per - 1 - 2 * step)

        def arrive(cc, i=i):
            index_from(i, cc)

        each(n_c, arrive)

        def to_owners(turn, i=i):
            owners = [exclusive(c, n_c - 1 - turn * batch - k, n_c) for k in range(batch)]
            for k, cc in enumerate(owners):
                degrid(i, cc, k)
            for k, cc in enumerate(owners):
                last = k == batch - 1
                send_vis(i, cc, last if not isinstance(turn, int) else last and turn == n_c // batch - 1)

        each(n_c // batch, to_owners)

    swap.wait_send()

    def index_sent(step):
        (rf, target), copy = to_reader(step)
        if isinstance(step, int) and step > 0:
            copy.wait_send()
            return

        @pl.when(away(rf, target))
        def _():
            copy.wait_send()

    def vis_sent(step):
        i, cc = lax.rem(step, per), lax.rem(c + step // per, n_c)
        if isinstance(step, int) and step >= per:
            vis_copy(i, cc).wait_send()
            return

        @pl.when(away(core * per + i, cc))
        def _():
            vis_copy(i, cc).wait_send()

    each(n_f * n_p, index_sent)
    each(per * n_c, vis_sent)

    def vis_from(step):
        sf, sp = step // n_p, lax.rem(step, n_p)
        pltpu.make_async_copy(vsend.at[0, 0], vrecv.at[sf, sp], vrecv_sem.at[sf, sp]).wait()

    each(n_f * n_p, vis_from)
    acc = jnp.zeros((2 * blocks, slots), F32)
    for sf in range(n_f):
        for sp in range(n_p):
            acc = acc + vrecv[sf, sp]
    for b in range(blocks):
        live = iota((1, slots), 1) < count_ref[b]
        vis_ref[b : b + 1] = jnp.where(live, acc[b : b + 1], 0.0)
        vis_ref[blocks + b : blocks + b + 1] = jnp.where(live, acc[blocks + b : blocks + b + 1], 0.0)


def local(sky_re, sky_im, col_offsets, sub_offsets, kernel, vis_count, cell_index, frac_index):
    n_f = lax.axis_size("facet")
    n_c = lax.axis_size("col")
    pixels, cols = sky_re.shape[1:]
    subs = sub_offsets.shape[0]
    owned, blocks = vis_count.shape
    slots = cell_index.shape[-1]
    over, ksize = kernel.shape
    assert owned == 1 and subs == n_f
    chunks = 4
    per = subs // SCOL
    n_p = n_c // SCOL
    batch = min(n_c, 4)
    dims = (n_f, n_c, pixels, cols, subs, blocks, slots, chunks, ksize, over)
    smem = pl.BlockSpec(memory_space=pltpu.SMEM)
    vmem = pl.BlockSpec(memory_space=pltpu.VMEM)
    anywhere = pl.BlockSpec(memory_space=pl.ANY)
    dma = pltpu.SemaphoreType.DMA
    vis = pl.pallas_call(
        functools.partial(body, dims),
        out_shape=jax.ShapeDtypeStruct((2 * blocks, slots), F32),
        in_specs=[smem, smem, smem, smem, vmem, vmem, anywhere, anywhere],
        out_specs=vmem,
        scratch_shapes=[
            pltpu.VMEM((2, pixels, cols), BF16),
            pltpu.VMEM((pixels, 2 * cols), BF16),
            pltpu.VMEM((2 * S, pixels), BF16),
            pltpu.VMEM((256, 256), BF16),
            pltpu.VMEM((2, 2 * S, LANES), F32),
            pltpu.VMEM((2, 2 * S, LANES), F32),
            pltpu.VMEM((2 * S, 2 * cols), F32),
            pltpu.VMEM((4, 64, LANES), F32),
            pltpu.VMEM((2, per, 8, SCOL * cols), F32),
            pltpu.VMEM((2, 8, S), F32),
            pltpu.VMEM((2 * S, SCOL * cols), BF16),
            pltpu.VMEM((per, 2 * S, SCOL * cols), BF16),
            pltpu.VMEM((SCOL, 2, S, cols), BF16),
            pltpu.VMEM((2, S, cols), BF16),
            pltpu.VMEM((per, 2 * S, S), BF16),
            pltpu.VMEM((4 * blocks, slots), BF16),
            pltpu.VMEM((per, n_c, 4 * blocks, slots), BF16),
            pltpu.VMEM((ksize, over, 2 * blocks, slots), F32),
            pltpu.VMEM((batch, ksize, 2 * blocks, slots), F32),
            pltpu.VMEM((batch, 2 * blocks, slots), jnp.int32),
            pltpu.VMEM((batch, blocks, 16, slots), BF16),
            pltpu.VMEM((batch, blocks, 16, slots), jnp.int16),
            pltpu.VMEM((batch, S, blocks * slots), BF16),
            pltpu.VMEM((per, n_c, 2 * blocks, slots), F32),
            pltpu.VMEM((n_f, n_p, 2 * blocks, slots), F32),
            dma((chunks, 4)),
            dma((2,)),
            dma((n_f, n_p)),
            dma((per, n_c)),
            dma((per, n_c)),
            dma((n_f, n_p)),
        ],
        compiler_params=pltpu.CompilerParams(
            collective_id=0, has_side_effects=True, vmem_limit_bytes=60 << 20
        ),
    )(
        col_offsets,
        sub_offsets,
        kernel.T,
        vis_count.reshape(blocks),
        cell_index.reshape(2 * blocks, slots),
        frac_index.reshape(2 * blocks, slots),
        sky_re,
        sky_im,
    )
    vis = vis.reshape(2, 1, blocks, slots)
    return (vis[0], vis[1])


def solution(mesh):
    placed = (
        P("facet", None, "col"),
        P("facet", None, "col"),
        P(),
        P(),
        P(),
        P("facet", "col"),
        P(None, "facet", "col", None),
        P(None, "facet", "col", None),
    )
    return jax.shard_map(
        local,
        mesh=mesh,
        in_specs=placed,
        out_specs=(P("facet", "col", None), P("facet", "col", None)),
        check_vma=False,
    )
```

```python
import functools
import math

import jax
import jax.numpy as jnp
from jax import lax
from jax.experimental import pallas as pl
from jax.experimental.pallas import tpu as pltpu
from jax.sharding import PartitionSpec as P

N_IMG = 65536
S = 256
SCOL = 2
LANES = 128
F32 = jnp.float32
BF16 = jnp.bfloat16


def iota(shape, dim):
    return lax.broadcasted_iota(jnp.int32, shape, dim)


def unit(points, period):
    quarter = period // 4
    quad = (points + quarter // 2) >> (quarter.bit_length() - 1)
    x = (points - quad * quarter).astype(F32) * (2.0 * math.pi / period)
    x2 = x * x
    s = x2 * (1.0 / 362880) - 1.0 / 5040
    s = x2 * s + 1.0 / 120
    s = x2 * s - 1.0 / 6
    s = x * (x2 * s + 1.0)
    c = x2 * (1.0 / 40320) - 1.0 / 720
    c = x2 * c + 1.0 / 24
    c = x2 * c - 0.5
    c = x2 * c + 1.0
    odd = (quad & 1) != 0
    cos = jnp.where(odd, s, c)
    sin = jnp.where(odd, c, s)
    cos = jnp.where(((quad + 1) & 2) != 0, -cos, cos)
    sin = jnp.where((quad & 2) != 0, -sin, sin)
    return cos, sin


def product(left, right, period):
    upper = (left * (right >> 8)) & (period - 1)
    return (upper * 256 + left * (right & 255)) & (period - 1)


def times(left, right):
    return (
        left[0] * right[0] - left[1] * right[1],
        left[0] * right[1] + left[1] * right[0],
    )


def exclusive(left, right, count):
    total, bit = 0, 1
    while bit < count:
        total = total + ((left // bit) % 2 + (right // bit) % 2) % 2 * bit
        bit *= 2
    return total


def each(count, step):
    if count <= 16:
        for index in range(count):
            step(index)
    else:

        def once(index, carry):
            step(index)
            return carry

        lax.fori_loop(0, count, once, 0)


def body(
    dims,
    coff_ref,
    soff_ref,
    kern_ref,
    count_ref,
    cell_ref,
    frac_ref,
    re_hbm,
    im_hbm,
    vis_ref,
    sky,
    folded,
    table,
    flip_mat,
    state,
    jumps,
    prod,
    base,
    shift_tab,
    turn_tab,
    table2,
    stacked,
    partial,
    bands,
    bsend,
    cells,
    idx,
    idx_all,
    kern_vec,
    tap_buf,
    cell_buf,
    row_buf,
    at_buf,
    weights,
    vsend,
    vrecv,
    sky_sem,
    band_sem,
    isend_sem,
    irecv_sem,
    vsend_sem,
    vrecv_sem,
):
    n_f, n_c, pixels, cols, subs, blocks, slots, chunks, ksize, over = dims
    per = subs // SCOL
    n_p = n_c // SCOL
    rows = 64
    f = lax.axis_index("facet")
    c = lax.axis_index("col")
    core = lax.rem(c, SCOL)
    chip = c // SCOL
    side = f // per
    depth = pixels // 2 // chunks
    wide = 2 * N_IMG

    loads = []
    for t in range(chunks):
        for k, start in enumerate((t * depth, pixels - (t + 1) * depth)):
            for index, src in enumerate((re_hbm, im_hbm)):
                copy = pltpu.make_async_copy(
                    src.at[0, pl.ds(start, depth)],
                    sky.at[index, pl.ds(start, depth)],
                    sky_sem.at[t, 2 * k + index],
                )
                copy.start()
                loads.append(copy)

    barrier = pltpu.get_barrier_semaphore()
    everyone = n_f * n_c

    def greet(step):
        other = lax.rem(f * n_c + c + 1 + step, everyone)
        pl.semaphore_signal(
            barrier, inc=1, device_id={"facet": other // n_c, "col": lax.rem(other, n_c)}
        )

    each(everyone - 1, greet)

    jrow = iota((rows, LANES), 0)
    twice = pixels - 1 - 2 * iota((rows, LANES), 1)
    base[0], base[1] = unit((jrow * twice) & (wide - 1), wide)
    base[2], base[3] = unit((jrow * (2 * LANES)) & (wide - 1), wide)
    scale1 = 1.0 / math.sqrt(pixels)
    order = (1 - core, core)

    def fill_table(t):
        for n, q in enumerate(order):
            for g in range(S // rows):
                start = coff_ref[q] + g * rows
                here = slice(n * S + g * rows, n * S + (g + 1) * rows)
                if t == 0:
                    ll = pixels - 1 - 2 * iota((8, LANES), 1)
                    jump = unit((start * (2 * LANES) + 0 * ll) & (wide - 1), wide)
                    jump = times((base[2], base[3]), (jump[0][0:1], jump[1][0:1]))
                    jump = (jump[0], -jump[1])
                    jumps[0, here], jumps[1, here] = jump
                    along = unit((start * ll) & (wide - 1), wide)
                    along = (along[0][0:1] * scale1, along[1][0:1] * scale1)
                    now = times((base[0], base[1]), along)
                else:
                    jump = (jumps[0, here], jumps[1, here])
                    now = (state[0, here], state[1, here])
                for part in range(depth // LANES):
                    lanes = slice(2 * t * depth + part * LANES, 2 * t * depth + (part + 1) * LANES)
                    table[here, lanes] = now[0].astype(BF16)
                    lanes = slice(lanes.start + depth, lanes.stop + depth)
                    table[here, lanes] = now[1].astype(BF16)
                    now = times(now, jump)
                if t + 1 < chunks:
                    state[0, here], state[1, here] = now

    tile = flip_mat.shape[0]
    flip_mat[...] = jnp.where(iota((tile, tile), 0) + iota((tile, tile), 1) == tile - 1, 1.0, 0.0).astype(BF16)

    def fold(t):
        for index in range(2):
            here = slice(index * cols, (index + 1) * cols)
            there = slice((1 - index) * cols, (2 - index) * cols)
            for k in range(0, depth, tile):
                high = sky[index, pixels - t * depth - k - tile : pixels - t * depth - k]
                high = jnp.dot(flip_mat[...], high, preferred_element_type=F32).astype(BF16)
                low = sky[index, t * depth + k : t * depth + k + tile]
                top = 2 * t * depth + k
                folded[top : top + tile, here] = low + high
                top = top + depth
                folded[top : top + tile, there] = low - high if index == 0 else high - low

    def finish(band, top):
        for index in range(2):
            band[index] = prod[top : top + S, index * cols : (index + 1) * cols].astype(BF16)

    first_y = f * pixels + chip * SCOL * cols
    scale2 = 1.0 / math.sqrt(pixels * n_f)

    def fill_second():
        for h, place in enumerate((core, 1 - core)):
            begin = first_y + place * cols
            for g in range(S // rows):
                k = iota((rows, LANES), 0) + g * rows
                y = begin + iota((rows, LANES), 1)
                now = unit(product(k, y, N_IMG), N_IMG)
                now = (now[0] * scale2, now[1] * scale2)
                jump = unit((k * LANES) & (N_IMG - 1), N_IMG)
                for part in range(cols // LANES):
                    lanes = slice(h * cols + part * LANES, h * cols + (part + 1) * LANES)
                    table2[g * rows : (g + 1) * rows, lanes] = now[0].astype(BF16)
                    table2[S + g * rows : S + (g + 1) * rows, lanes] = now[1].astype(BF16)
                    now = times(now, jump)
            for i in range(per):
                at = slice(h * cols, (h + 1) * cols)
                y = begin + iota((8, cols), 1)
                turn = unit(product(soff_ref[core * per + i], y, N_IMG), N_IMG)
                shift_tab[0, i, :, at], shift_tab[1, i, :, at] = turn
        j = coff_ref[core] + iota((8, S), 1)
        turn_tab[0], turn_tab[1] = unit((j * (pixels - 1)) & (wide - 1), wide)

    both_index = jnp.concatenate([cell_ref[...], frac_ref[...]], axis=0)
    idx[...] = both_index.astype(F32).astype(BF16)

    def away(facet, col):
        return jnp.logical_or(facet != f, col != c)

    own_index = idx_all.at[lax.rem(f, per), c]
    own_sem = irecv_sem.at[lax.rem(f, per), c]

    def to_reader(step):
        rf = lax.rem(f + step // n_p, n_f)
        rp = lax.rem(chip + lax.rem(step, n_p), n_p)
        target = rp * SCOL + side
        return (rf, target), pltpu.make_async_remote_copy(
            src_ref=idx,
            dst_ref=own_index,
            send_sem=isend_sem.at[rf, rp],
            recv_sem=own_sem,
            device_id={"facet": rf, "col": target},
        )

    def send_index(step):
        (rf, target), copy = to_reader(step)
        if isinstance(step, int) and step > 0:
            copy.start()
            return

        @pl.when(away(rf, target))
        def _():
            copy.start()

        @pl.when(jnp.logical_not(away(rf, target)))
        def _():
            pltpu.make_async_copy(idx, own_index, own_sem).start()

    other = 1 - core
    def landed(t):
        for copy in loads[4 * t : 4 * t + 4]:
            copy.wait()

    for tap in range(ksize):
        for step in range(over):
            kern_vec[tap, step] = jnp.full((2 * blocks, slots), kern_ref[tap, step], F32)

    split = chunks // 2
    fill_table(0)
    fill_second()
    landed(0)
    fold(0)
    fill_table(1)
    for t in range(chunks):
        if t + 1 < chunks:
            landed(t + 1)
            fold(t + 1)
        if 0 < t < chunks - 1:
            fill_table(t + 1)
        here = slice(2 * t * depth, 2 * (t + 1) * depth)
        lines = slice(0, S if t >= split else 2 * S)
        for index in range(2):
            at = slice(index * cols, (index + 1) * cols)
            term = jnp.dot(table[lines, here], folded[here, at], preferred_element_type=F32)
            if t == 0:
                prod[lines, at] = term
            else:
                prod[lines, at] += term
        if t == chunks // 2 - 1:
            pl.semaphore_wait(barrier, everyone - 1)
            each(n_f * n_p, send_index)

    finish(bsend, 0)
    swap = pltpu.make_async_remote_copy(
        src_ref=bsend,
        dst_ref=bands.at[1],
        send_sem=band_sem.at[0],
        recv_sem=band_sem.at[1],
        device_id={"facet": f, "col": chip * SCOL + other},
    )

    swap.start()

    def index_from(i, cc):
        pltpu.make_async_copy(idx, idx_all.at[i, cc], irecv_sem.at[i, cc]).wait()

    sub = iota((8, slots), 0)

    sub16 = iota((16, slots), 0)

    def prepare(i, cc, slot):
        block = idx_all[i, cc].astype(F32).astype(jnp.int32)
        frac = block[2 * blocks :]
        cell_buf[slot] = block[: 2 * blocks]
        for tap in range(ksize):
            values = [kern_vec[tap, step] for step in range(over)]
            bit = 1
            while len(values) > 1:
                odd = (frac & bit) != 0
                values = [jnp.where(odd, high, low) for low, high in zip(values[::2], values[1::2])]
                bit *= 2
            tap_buf[slot, tap] = values[0]

        def window(b, line):
            size = line.shape[0]
            cell = jnp.broadcast_to(cell_buf[slot, b : b + 1], line.shape)
            lo = cell & (size - 1)
            turn = (line - lo) & (size - 1)
            value = jnp.zeros(line.shape, F32)
            for tap in range(ksize):
                value = jnp.where(turn == tap, tap_buf[slot, tap, b : b + 1], value)
            high = cell >> (size.bit_length() - 1)
            return value, high + jnp.where(line < lo, 1, 0)

        for b in range(blocks):
            value, at = window(b, sub16)
            row_buf[slot, b] = value.astype(BF16)
            at_buf[slot, b] = at.astype(jnp.int16)
        return [window(blocks + b, sub) for b in range(blocks)]

    here = slice(2 * split * depth, pixels)
    for index in range(2):
        at = slice(index * cols, (index + 1) * cols)
        prod[S:, at] += jnp.dot(table[S:, here], folded[here, at], preferred_element_type=F32)
    finish(bands.at[0], S)

    def shift(h, step=16):
        for part in range(cols // LANES):
            near = slice(part * LANES, (part + 1) * LANES)
            at = slice(h * cols + near.start, h * cols + near.stop)
            for top in range(0, S, step):
                re = bands[h, 0, top : top + step, near].astype(F32)
                im = bands[h, 1, top : top + step, near].astype(F32)
                for i in range(per):
                    sc = shift_tab[0, i, 0:1, at]
                    sd = shift_tab[1, i, 0:1, at]
                    stacked[i, top : top + step, at] = (re * sc + im * sd).astype(BF16)
                    stacked[i, S + top : S + top + step, at] = (im * sc - re * sd).astype(BF16)

    def term_of(i, h):
        at = slice(h * cols, (h + 1) * cols)
        return lax.dot_general(
            table2[:, at], stacked[i, :, at], (((1,), (1,)), ((), ())), preferred_element_type=F32
        )

    shift(0)
    for i in range(per):
        partial[i] = term_of(i, 0)
    swap.wait_recv()
    shift(1)

    def grid_of(i):
        both = partial[i] + term_of(i, 1)
        re = both[:S, :S] + both[S:, S:]
        im = both[:S, S:] - both[S:, :S]
        tc, td = turn_tab[0, 0:1], turn_tab[1, 0:1]
        cells[i, :S] = (re * tc + im * td).astype(BF16)
        cells[i, S:] = (im * tc - re * td).astype(BF16)

    for i in range(per):
        grid_of(i)

    def vis_copy(i, cc):
        return pltpu.make_async_remote_copy(
            src_ref=vsend.at[i, cc],
            dst_ref=vrecv.at[f, chip],
            send_sem=vsend_sem.at[i, cc],
            recv_sem=vrecv_sem.at[f, chip],
            device_id={"facet": core * per + i, "col": cc},
        )

    def degrid(i, cc, slot):
        col = prepare(i, cc, slot)
        for b in range(blocks):
            lanes = slice(b * slots, (b + 1) * slots)
            value, at = row_buf[slot, b], at_buf[slot, b]
            for g in range(S // 16):
                weights[slot, 16 * g : 16 * (g + 1), lanes] = jnp.where(
                    at == jnp.int16(g), value, jnp.zeros_like(value)
                )
        summed = jnp.dot(cells[i], weights[slot], preferred_element_type=F32)
        for b in range(blocks):
            lanes = slice(b * slots, (b + 1) * slots)
            value, at = col[b]
            acc_re = acc_im = jnp.zeros((8, slots), F32)
            for g in range(S // 8):
                hit = at == g
                acc_re = jnp.where(hit, summed[8 * g : 8 * g + 8, lanes], acc_re)
                acc_im = jnp.where(hit, summed[S + 8 * g : S + 8 * g + 8, lanes], acc_im)
            vsend[i, cc, b : b + 1] = jnp.sum(value * acc_re, axis=0, keepdims=True)
            vsend[i, cc, blocks + b : blocks + b + 1] = jnp.sum(value * acc_im, axis=0, keepdims=True)

    def send_vis(i, cc, near):
        if not near:
            vis_copy(i, cc).start()
            return

        @pl.when(away(core * per + i, cc))
        def _():
            vis_copy(i, cc).start()

        @pl.when(jnp.logical_not(away(core * per + i, cc)))
        def _():
            pltpu.make_async_copy(vsend.at[i, cc], vrecv.at[f, chip], vrecv_sem.at[f, chip]).start()

    flip = jnp.where(f < core * per + per // 2, 1, 0)
    batch = min(n_c, 4)
    for step in range(per):
        i = step + flip * (per - 1 - 2 * step)

        def arrive(cc, i=i):
            index_from(i, cc)

        each(n_c, arrive)

        def to_owners(turn, i=i):
            owners = [exclusive(c, n_c - 1 - turn * batch - k, n_c) for k in range(batch)]
            for k, cc in enumerate(owners):
                degrid(i, cc, k)
            for k, cc in enumerate(owners):
                last = k == batch - 1
                send_vis(i, cc, last if not isinstance(turn, int) else last and turn == n_c // batch - 1)

        each(n_c // batch, to_owners)

    swap.wait_send()

    def index_sent(step):
        (rf, target), copy = to_reader(step)
        if isinstance(step, int) and step > 0:
            copy.wait_send()
            return

        @pl.when(away(rf, target))
        def _():
            copy.wait_send()

    def vis_sent(step):
        i, cc = lax.rem(step, per), lax.rem(c + step // per, n_c)
        if isinstance(step, int) and step >= per:
            vis_copy(i, cc).wait_send()
            return

        @pl.when(away(core * per + i, cc))
        def _():
            vis_copy(i, cc).wait_send()

    each(n_f * n_p, index_sent)
    each(per * n_c, vis_sent)

    def vis_from(step):
        sf, sp = step // n_p, lax.rem(step, n_p)
        pltpu.make_async_copy(vsend.at[0, 0], vrecv.at[sf, sp], vrecv_sem.at[sf, sp]).wait()

    each(n_f * n_p, vis_from)
    acc = jnp.zeros((2 * blocks, slots), F32)
    for sf in range(n_f):
        for sp in range(n_p):
            acc = acc + vrecv[sf, sp]
    for b in range(blocks):
        live = iota((1, slots), 1) < count_ref[b]
        vis_ref[b : b + 1] = jnp.where(live, acc[b : b + 1], 0.0)
        vis_ref[blocks + b : blocks + b + 1] = jnp.where(live, acc[blocks + b : blocks + b + 1], 0.0)


def local(sky_re, sky_im, col_offsets, sub_offsets, kernel, vis_count, cell_index, frac_index):
    n_f = lax.axis_size("facet")
    n_c = lax.axis_size("col")
    pixels, cols = sky_re.shape[1:]
    subs = sub_offsets.shape[0]
    owned, blocks = vis_count.shape
    slots = cell_index.shape[-1]
    over, ksize = kernel.shape
    assert owned == 1 and subs == n_f
    chunks = 4
    per = subs // SCOL
    n_p = n_c // SCOL
    batch = min(n_c, 4)
    dims = (n_f, n_c, pixels, cols, subs, blocks, slots, chunks, ksize, over)
    smem = pl.BlockSpec(memory_space=pltpu.SMEM)
    vmem = pl.BlockSpec(memory_space=pltpu.VMEM)
    anywhere = pl.BlockSpec(memory_space=pl.ANY)
    dma = pltpu.SemaphoreType.DMA
    vis = pl.pallas_call(
        functools.partial(body, dims),
        out_shape=jax.ShapeDtypeStruct((2 * blocks, slots), F32),
        in_specs=[smem, smem, smem, smem, vmem, vmem, anywhere, anywhere],
        out_specs=vmem,
        scratch_shapes=[
            pltpu.VMEM((2, pixels, cols), BF16),
            pltpu.VMEM((pixels, 2 * cols), BF16),
            pltpu.VMEM((2 * S, pixels), BF16),
            pltpu.VMEM((256, 256), BF16),
            pltpu.VMEM((2, 2 * S, LANES), F32),
            pltpu.VMEM((2, 2 * S, LANES), F32),
            pltpu.VMEM((2 * S, 2 * cols), F32),
            pltpu.VMEM((4, 64, LANES), F32),
            pltpu.VMEM((2, per, 8, SCOL * cols), F32),
            pltpu.VMEM((2, 8, S), F32),
            pltpu.VMEM((2 * S, SCOL * cols), BF16),
            pltpu.VMEM((per, 2 * S, SCOL * cols), BF16),
            pltpu.VMEM((per, 2 * S, 2 * S), F32),
            pltpu.VMEM((SCOL, 2, S, cols), BF16),
            pltpu.VMEM((2, S, cols), BF16),
            pltpu.VMEM((per, 2 * S, S), BF16),
            pltpu.VMEM((4 * blocks, slots), BF16),
            pltpu.VMEM((per, n_c, 4 * blocks, slots), BF16),
            pltpu.VMEM((ksize, over, 2 * blocks, slots), F32),
            pltpu.VMEM((batch, ksize, 2 * blocks, slots), F32),
            pltpu.VMEM((batch, 2 * blocks, slots), jnp.int32),
            pltpu.VMEM((batch, blocks, 16, slots), BF16),
            pltpu.VMEM((batch, blocks, 16, slots), jnp.int16),
            pltpu.VMEM((batch, S, blocks * slots), BF16),
            pltpu.VMEM((per, n_c, 2 * blocks, slots), F32),
            pltpu.VMEM((n_f, n_p, 2 * blocks, slots), F32),
            dma((chunks, 4)),
            dma((2,)),
            dma((n_f, n_p)),
            dma((per, n_c)),
            dma((per, n_c)),
            dma((n_f, n_p)),
        ],
        compiler_params=pltpu.CompilerParams(
            collective_id=0, has_side_effects=True, vmem_limit_bytes=60 << 20
        ),
    )(
        col_offsets,
        sub_offsets,
        kernel.T,
        vis_count.reshape(blocks),
        cell_index.reshape(2 * blocks, slots),
        frac_index.reshape(2 * blocks, slots),
        sky_re,
        sky_im,
    )
    vis = vis.reshape(2, 1, blocks, slots)
    return (vis[0], vis[1])


def solution(mesh):
    placed = (
        P("facet", None, "col"),
        P("facet", None, "col"),
        P(),
        P(),
        P(),
        P("facet", "col"),
        P(None, "facet", "col", None),
        P(None, "facet", "col", None),
    )
    return jax.shard_map(
        local,
        mesh=mesh,
        in_specs=placed,
        out_specs=(P("facet", "col", None), P("facet", "col", None)),
        check_vma=False,
    )
```
